256 devices in a mesh: dom: 64 (over x, z, y_hi), head: 4 (over y_lo, core).
Axes of the slice: x: 4, y: 4 (y_hi: 2, y_lo: 2; y = y_hi * 2 + y_lo), z: 8, core: 2. Of those that a mesh axis runs over, the one named last changes fastest.
Arguments:
- vertex_embeddings: bfloat16 [32768, 512], P(('dom', 'head')), may hold values from -6 to 6
- adjacent_group_bank_ids: int32 [64, 4, 12], P('dom', 'head'), may hold values from -1 to 15, as said below
- coupling_strength_panels: bfloat16 [16, 128, 128], replicated, may hold values from -0.3125 to 0.3125
- asking_projector: bfloat16 [512, 512], replicated, may hold values from -0.25 to 0.25
- lookup_projector: bfloat16 [512, 512], replicated, may hold values from -0.25 to 0.25
- content_projector: bfloat16 [512, 512], replicated, may hold values from -0.25 to 0.25
- final_projector: bfloat16 [512, 512], replicated, may hold values from -0.25 to 0.25
- passing_inner_coefficients: bfloat16 [512, 1024], replicated, may hold values from -0.25 to 0.25
- passing_outer_coefficients: bfloat16 [1024, 512], replicated, may hold values from -0.1875 to 0.1875
- softness_per_subspace: float32 [8], replicated, may hold values from 0.5 to 2
- mixing_layer_gain: float32 [512], replicated, may hold values from 0.5 to 1.5
Outputs:
- result: bfloat16 [32768, 512], P(('dom', 'head'))
The draws below stay inside these ranges and needn't reach their ends.
Inputs may be any that keep to these rules, and one draw needn't show every extreme that they name: `adjacent_group_bank_ids`: -1 marks a block without edges. The entry of a block for itself is never -1, nor is at least one entry for each neighbouring partition.
All inputs are finite; a program needn't handle non-finite values.
Results may differ from the reference program's by a relative error of at most 0.0054.
Values may be sent and summed in bfloat16 or wider, within the bound.
A program may use at most 64 MiB of HBM per device.

```python
import math
import jax
import jax.numpy as jnp
from jax import lax

D = 512
NUM_SUBSPACES = 8
SUBSPACE_WIDTH = 64
FF = 1024
TILES = 16
NODE_DEV = 128
PART = 512
NODES = 32768
N_DOM = 64
N_HEAD = 4


def draw_adjacent_group_bank_ids(key, part):
    key_listed, key_tile, key_left, key_right = jax.random.split(key, 4)
    shape = (N_DOM, N_HEAD, 3 * N_HEAD)
    listed = jax.random.randint(key_listed, shape, 0, 5) < 2
    tile_ids = jax.random.randint(key_tile, shape, 0, TILES)
    pick_left = jax.random.randint(key_left, (N_DOM, N_HEAD, 1), 0, N_HEAD)
    pick_right = jax.random.randint(key_right, (N_DOM, N_HEAD, 1), 0, N_HEAD)
    slots = jnp.arange(3 * N_HEAD)[None, None, :]
    own_slot = slots == (N_HEAD + jnp.arange(N_HEAD))[None, :, None]
    forced = own_slot | (slots == pick_left) | (slots == 2 * N_HEAD + pick_right)
    return jnp.where(listed | forced, tile_ids, -1).astype(jnp.int32)


def block_levels(own_key, extent, cuts, low, largest):
    def one(dim, parts):
        heights = jax.random.uniform(jax.random.fold_in(jax.random.fold_in(own_key, 6), dim), (parts,), jnp.float32, low / len(cuts), largest / len(cuts))
        return jnp.repeat(jnp.exp(heights), extent[dim] // parts).reshape((-1,) + (1,) * (len(extent) - dim - 1))

    loudness = one(*cuts[0])
    for cut in cuts[1:]:
        loudness = loudness * one(*cut)
    return loudness


def scatter_about(stream_key, extent, width, limit, cuts=(), held_as=jnp.bfloat16):
    values = width * jax.random.normal(stream_key, extent, jnp.float32)
    if cuts:
        values = values * block_levels(stream_key, extent, cuts, -0.22, 0.18)
    return jnp.clip(values, -limit, limit).astype(held_as)


def setup_inputs(seed: int = 0) -> dict:
    key_list = jax.random.split(jax.random.key(seed), 12)
    return {
        "vertex_embeddings": scatter_about(key_list[0], (NODES, D), 1.0, 6.0, ((0, 256),)),
        "adjacent_group_bank_ids": draw_adjacent_group_bank_ids(jax.random.fold_in(key_list[11], 71), 0),
        "coupling_strength_panels": scatter_about(key_list[2], (TILES, NODE_DEV, NODE_DEV), (3 * NODE_DEV) ** -0.5, 0.3125),
        "asking_projector": scatter_about(key_list[3], (D, D), D ** -0.5, 0.25),
        "lookup_projector": scatter_about(key_list[4], (D, D), D ** -0.5, 0.25),
        "content_projector": scatter_about(key_list[5], (D, D), D ** -0.5, 0.25),
        "final_projector": scatter_about(key_list[6], (D, D), D ** -0.5, 0.25),
        "passing_inner_coefficients": scatter_about(key_list[7], (D, FF), D ** -0.5, 0.25),
        "passing_outer_coefficients": scatter_about(key_list[8], (FF, D), FF ** -0.5, 0.1875),
        "softness_per_subspace": jnp.clip(jnp.exp(jax.random.uniform(key_list[9], (NUM_SUBSPACES,), jnp.float32, math.log(0.5), math.log(2.0))), 0.5, 2.0),
        "mixing_layer_gain": jnp.clip(1.0 + 0.1 * jax.random.normal(key_list[10], (D,), jnp.float32), 0.5, 1.5),
    }


norm_eps = 1e-06

def head_norm(projected, scales):
    grouped = projected.reshape(projected.shape[0], NUM_SUBSPACES, SUBSPACE_WIDTH)
    mean_square = lax.optimization_barrier(jnp.mean(grouped * grouped, axis=-1, keepdims=True))
    scaled = grouped * lax.rsqrt(mean_square + norm_eps) * scales
    return scaled.reshape(projected.shape[0], D).astype(jnp.bfloat16)

def reference(vertex_embeddings, adjacent_group_bank_ids, coupling_strength_panels, asking_projector, lookup_projector, content_projector, final_projector, passing_inner_coefficients, passing_outer_coefficients, softness_per_subspace, mixing_layer_gain):
    block_len = NODE_DEV
    blocks = vertex_embeddings.reshape(N_DOM, N_HEAD, block_len, D)
    zero_pad = jnp.zeros((1, N_HEAD, block_len, D), vertex_embeddings.dtype)
    padded = jnp.concatenate([zero_pad, blocks, zero_pad], axis=0)
    link_rows = adjacent_group_bank_ids.reshape(N_DOM * N_HEAD, 3 * N_HEAD)

    def block_message(device_id):
        part_index = (device_id // N_HEAD).astype(jnp.int32)
        nearby = lax.dynamic_slice_in_dim(padded, part_index, 3, 0).reshape(3 * N_HEAD * block_len, D)
        slot_ids = link_rows[device_id]
        selected = jnp.take(coupling_strength_panels, jnp.maximum(slot_ids, 0), axis=0)
        selected = jnp.where((slot_ids >= 0)[:, None, None], selected, jnp.zeros_like(selected))
        wide_tiles = jnp.transpose(selected, (1, 0, 2)).reshape(block_len, 3 * N_HEAD * block_len)
        return jnp.dot(wide_tiles, nearby, preferred_element_type=jnp.float32).astype(jnp.bfloat16)
    aggregate = lax.map(block_message, jnp.arange(N_DOM * N_HEAD, dtype=jnp.int32)).reshape(NODES, D)
    hidden = jax.nn.gelu(jnp.dot(aggregate, passing_inner_coefficients, preferred_element_type=jnp.float32)).astype(jnp.bfloat16)
    local_term = jnp.dot(hidden, passing_outer_coefficients, preferred_element_type=jnp.float32)
    asking_vector_multiplier = (softness_per_subspace / math.sqrt(SUBSPACE_WIDTH))[None, :, None]
    queries = head_norm(jnp.dot(vertex_embeddings, asking_projector, preferred_element_type=jnp.float32), asking_vector_multiplier)
    keys_all = head_norm(jnp.dot(vertex_embeddings, lookup_projector, preferred_element_type=jnp.float32), jnp.ones((1, NUM_SUBSPACES, 1), jnp.float32))
    values_all = jnp.dot(vertex_embeddings, content_projector, preferred_element_type=jnp.float32).astype(jnp.bfloat16)

    def attend(query_block):
        pieces = []
        for head_id in range(NUM_SUBSPACES):
            cols = slice(head_id * SUBSPACE_WIDTH, (head_id + 1) * SUBSPACE_WIDTH)
            scores = jnp.dot(query_block[:, cols], keys_all[:, cols].T, preferred_element_type=jnp.float32)
            weights = jnp.exp(scores).astype(jnp.bfloat16)
            denominator = lax.optimization_barrier(jnp.sum(weights, axis=1, keepdims=True, dtype=jnp.float32))
            numerator = jnp.dot(weights, values_all[:, cols], preferred_element_type=jnp.float32)
            pieces.append((numerator / denominator).astype(jnp.bfloat16))
        return jnp.concatenate(pieces, axis=1)
    mixed = lax.map(attend, queries.reshape(NODES // PART, PART, D)).reshape(NODES, D)
    attended = jnp.dot(mixed, final_projector, preferred_element_type=jnp.float32)
    normed = attended * lax.rsqrt(lax.optimization_barrier(jnp.mean(attended * attended, axis=-1, keepdims=True)) + norm_eps) * mixing_layer_gain
    return (vertex_embeddings.astype(jnp.float32) + local_term + normed).astype(jnp.bfloat16)
```

```python
import math

import jax
import jax.numpy as jnp
from jax import lax
from jax.sharding import Mesh
from jax.sharding import PartitionSpec as P

NUM_SUBSPACES = 8
SUBSPACE_WIDTH = 64
KEY_BLOCK = 2048

norm_eps = 1e-06

PLANE = "xz"
PAIR = "yhi"
DOM = (PLANE, PAIR)
GROUP = (PAIR, "head")


def extended(shard, width):
    devices = lax.axis_size(PLANE) * lax.axis_size(PAIR)
    length = shard.shape[0]
    up = [(i, (i + 1) % devices) for i in range(devices - 1)]
    down = [(j, i) for i, j in up]
    last = lax.slice_in_dim(shard, length - width, length, axis=0)
    first = lax.slice_in_dim(shard, 0, width, axis=0)
    before = lax.ppermute(last, DOM, up)
    after = lax.ppermute(first, DOM, down)
    return jnp.concatenate([before, shard, after], axis=0)


def head_norm(projected, scales):
    rows = projected.shape[0]
    grouped = projected.reshape(rows, -1, SUBSPACE_WIDTH)
    mean_square = jnp.mean(grouped * grouped, axis=-1, keepdims=True)
    scaled = grouped * lax.rsqrt(mean_square + norm_eps)
    if scales is not None:
        scaled = scaled * scales[None, :, None]
    return scaled.reshape(rows, -1).astype(jnp.bfloat16)


def shards(
    vertex_embeddings,
    adjacent_group_bank_ids,
    coupling_strength_panels,
    asking_projector,
    lookup_projector,
    content_projector,
    final_projector,
    passing_inner_coefficients,
    passing_outer_coefficients,
    softness_per_subspace,
    mixing_layer_gain,
):
    block_len = vertex_embeddings.shape[0]
    group_size = lax.axis_size("head")
    pair_size = lax.axis_size(PAIR)
    members = group_size * pair_size
    slot_ids = adjacent_group_bank_ids.reshape(-1)
    halo_rows = extended(vertex_embeddings, block_len)
    nearby = lax.all_gather(halo_rows, "head", axis=0, tiled=True)
    slot_order = slot_ids.reshape(3, group_size).T.reshape(-1)
    asking_vector_multiplier = softness_per_subspace / math.sqrt(SUBSPACE_WIDTH)
    queries = head_norm(
        jnp.dot(vertex_embeddings, asking_projector, preferred_element_type=jnp.float32),
        asking_vector_multiplier,
    )
    keys_all = head_norm(
        jnp.dot(vertex_embeddings, lookup_projector, preferred_element_type=jnp.float32), None
    )
    values_all = jnp.dot(
        vertex_embeddings, content_projector, preferred_element_type=jnp.float32
    ).astype(jnp.bfloat16)

    head_of = [(j % group_size) * pair_size + j // group_size for j in range(members)]
    member_of = [head_of.index(h) for h in range(NUM_SUBSPACES)]
    packed = jnp.stack(
        [t.reshape(block_len, NUM_SUBSPACES, SUBSPACE_WIDTH) for t in (queries, keys_all, values_all)],
        axis=2,
    )[:, jnp.array(head_of)]
    packed = packed.reshape(block_len, -1)
    mine = lax.all_to_all(packed, GROUP, split_axis=1, concat_axis=0, tiled=True)
    query_rows = mine.shape[0]
    head_queries = mine[:, :SUBSPACE_WIDTH]
    key_values = mine[:, SUBSPACE_WIDTH:]

    selected = jnp.take(coupling_strength_panels, jnp.maximum(slot_order, 0), axis=0)
    selected = jnp.where((slot_order >= 0)[:, None, None], selected, jnp.zeros_like(selected))
    wide_tiles = jnp.transpose(selected, (1, 0, 2)).reshape(block_len, -1)
    aggregate = jnp.dot(wide_tiles, nearby, preferred_element_type=jnp.float32).astype(jnp.bfloat16)
    hidden = jax.nn.gelu(
        jnp.dot(aggregate, passing_inner_coefficients, preferred_element_type=jnp.float32)
    ).astype(jnp.bfloat16)
    local_term = jnp.dot(hidden, passing_outer_coefficients, preferred_element_type=jnp.float32)

    kv_in = lax.all_gather(key_values, PLANE, axis=0, tiled=True)
    key_count = kv_in.shape[0]
    block_step = min(KEY_BLOCK, key_count)
    ones = jnp.ones((block_step, SUBSPACE_WIDTH), jnp.bfloat16)

    def accumulate(turn_index, totals):
        block = lax.dynamic_slice_in_dim(kv_in, turn_index * block_step, block_step, 0)
        scores = jnp.einsum(
            "qd,kd->qk",
            head_queries,
            block[:, :SUBSPACE_WIDTH],
            preferred_element_type=jnp.float32,
        )
        weights = jnp.exp(scores).astype(jnp.bfloat16)
        widened = jnp.concatenate([block[:, SUBSPACE_WIDTH:], ones], axis=1)
        return totals + jnp.dot(weights, widened, preferred_element_type=jnp.float32)

    totals = lax.fori_loop(
        0,
        key_count // block_step,
        accumulate,
        jnp.zeros((query_rows, 2 * SUBSPACE_WIDTH), jnp.float32),
    )
    merged = (totals[:, :SUBSPACE_WIDTH] / totals[:, SUBSPACE_WIDTH : SUBSPACE_WIDTH + 1]).astype(
        jnp.bfloat16
    )
    back = lax.all_to_all(merged, GROUP, split_axis=0, concat_axis=1, tiled=True)
    node_heads = back.reshape(block_len, members, SUBSPACE_WIDTH)[:, jnp.array(member_of)]
    node_heads = node_heads.reshape(block_len, -1)
    attended = jnp.dot(node_heads, final_projector, preferred_element_type=jnp.float32)
    normed = (
        attended
        * lax.rsqrt(jnp.mean(attended * attended, axis=-1, keepdims=True) + norm_eps)
        * mixing_layer_gain
    )
    return (vertex_embeddings.astype(jnp.float32) + local_term + normed).astype(jnp.bfloat16)


def solution(mesh):
    n_dom, n_head = mesh.shape["dom"], mesh.shape["head"]
    fine = Mesh(mesh.devices.reshape(n_dom // 2, 2, n_head), (PLANE, PAIR, "head"))
    in_specs = (
        P((PLANE, PAIR, "head"), None),
        P(DOM, "head", None),
        P(),
        P(),
        P(),
        P(),
        P(),
        P(),
        P(),
        P(),
        P(),
    )
    out_specs = P((PLANE, PAIR, "head"), None)
    return jax.shard_map(shards, mesh=fine, in_specs=in_specs, out_specs=out_specs, check_vma=False)
```

```python
import math

import jax
import jax.numpy as jnp
from jax import lax
from jax.sharding import Mesh
from jax.sharding import PartitionSpec as P

NUM_SUBSPACES = 8
SUBSPACE_WIDTH = 64
KEY_BLOCK = 2048
KV_PIECES = 4

norm_eps = 1e-06

PLANE = "xz"
PAIR = "yhi"
DOM = (PLANE, PAIR)
GROUP = (PAIR, "head")


def extended(shard, width):
    devices = lax.axis_size(PLANE) * lax.axis_size(PAIR)
    length = shard.shape[0]
    up = [(i, (i + 1) % devices) for i in range(devices - 1)]
    down = [(j, i) for i, j in up]
    last = lax.slice_in_dim(shard, length - width, length, axis=0)
    first = lax.slice_in_dim(shard, 0, width, axis=0)
    before = lax.ppermute(last, DOM, up)
    after = lax.ppermute(first, DOM, down)
    return jnp.concatenate([before, shard, after], axis=0)


def head_norm(projected, scales):
    rows = projected.shape[0]
    grouped = projected.reshape(rows, -1, SUBSPACE_WIDTH)
    mean_square = jnp.mean(grouped * grouped, axis=-1, keepdims=True)
    scaled = grouped * lax.rsqrt(mean_square + norm_eps)
    if scales is not None:
        scaled = scaled * scales[None, :, None]
    return scaled.reshape(rows, -1).astype(jnp.bfloat16)


def shards(
    vertex_embeddings,
    adjacent_group_bank_ids,
    coupling_strength_panels,
    asking_projector,
    lookup_projector,
    content_projector,
    final_projector,
    passing_inner_coefficients,
    passing_outer_coefficients,
    softness_per_subspace,
    mixing_layer_gain,
):
    block_len = vertex_embeddings.shape[0]
    group_size = lax.axis_size("head")
    pair_size = lax.axis_size(PAIR)
    members = group_size * pair_size
    slot_ids = adjacent_group_bank_ids.reshape(-1)
    halo_rows = extended(vertex_embeddings, block_len)
    me = lax.axis_index("head")
    gathered = [halo_rows]
    for shift in range(1, group_size):
        pairs = [(i, (i + shift) % group_size) for i in range(group_size)]
        gathered.append(lax.ppermute(halo_rows, "head", pairs))
    stacked = jnp.stack(gathered)
    order = (me - jnp.arange(group_size)) % group_size
    nearby = jnp.zeros_like(stacked).at[order].set(stacked).reshape(-1, halo_rows.shape[1])
    slot_order = slot_ids.reshape(3, group_size).T.reshape(-1)
    asking_vector_multiplier = softness_per_subspace / math.sqrt(SUBSPACE_WIDTH)
    queries = head_norm(
        jnp.dot(vertex_embeddings, asking_projector, preferred_element_type=jnp.float32),
        asking_vector_multiplier,
    )
    keys_all = head_norm(
        jnp.dot(vertex_embeddings, lookup_projector, preferred_element_type=jnp.float32), None
    )
    values_all = jnp.dot(
        vertex_embeddings, content_projector, preferred_element_type=jnp.float32
    ).astype(jnp.bfloat16)

    head_of = [(j % group_size) * pair_size + j // group_size for j in range(members)]
    member_of = [head_of.index(h) for h in range(NUM_SUBSPACES)]
    packed = jnp.stack(
        [t.reshape(block_len, NUM_SUBSPACES, SUBSPACE_WIDTH) for t in (queries, keys_all, values_all)],
        axis=2,
    )[:, jnp.array(head_of)]
    packed = packed.reshape(block_len, -1)
    mine = lax.all_to_all(packed, GROUP, split_axis=1, concat_axis=0, tiled=True)
    query_rows = mine.shape[0]
    head_queries = mine[:, :SUBSPACE_WIDTH]
    key_values = mine[:, SUBSPACE_WIDTH:]

    selected = jnp.take(coupling_strength_panels, jnp.maximum(slot_order, 0), axis=0)
    selected = jnp.where((slot_order >= 0)[:, None, None], selected, jnp.zeros_like(selected))
    wide_tiles = jnp.transpose(selected, (1, 0, 2)).reshape(block_len, -1)
    aggregate = jnp.dot(wide_tiles, nearby, preferred_element_type=jnp.float32).astype(jnp.bfloat16)
    hidden = jax.nn.gelu(
        jnp.dot(aggregate, passing_inner_coefficients, preferred_element_type=jnp.float32)
    ).astype(jnp.bfloat16)
    local_term = jnp.dot(hidden, passing_outer_coefficients, preferred_element_type=jnp.float32)

    local_term, head_queries = lax.optimization_barrier((local_term, head_queries))
    piece_rows = query_rows // KV_PIECES
    totals = jnp.zeros((query_rows, 2 * SUBSPACE_WIDTH), jnp.float32)
    for piece in range(KV_PIECES):
        kv_in = lax.all_gather(
            key_values[piece * piece_rows : (piece + 1) * piece_rows], PLANE, axis=0, tiled=True
        )
        key_count = kv_in.shape[0]
        block_step = min(KEY_BLOCK, key_count)
        ones = jnp.ones((block_step, SUBSPACE_WIDTH), jnp.bfloat16)

        def accumulate(turn_index, totals, kv_in=kv_in, block_step=block_step, ones=ones):
            block = lax.dynamic_slice_in_dim(kv_in, turn_index * block_step, block_step, 0)
            scores = jnp.einsum(
                "qd,kd->qk",
                head_queries,
                block[:, :SUBSPACE_WIDTH],
                preferred_element_type=jnp.float32,
            )
            weights = jnp.exp(scores).astype(jnp.bfloat16)
            widened = jnp.concatenate([block[:, SUBSPACE_WIDTH:], ones], axis=1)
            return totals + jnp.dot(weights, widened, preferred_element_type=jnp.float32)

        totals = lax.fori_loop(0, key_count // block_step, accumulate, totals)
    merged = (totals[:, :SUBSPACE_WIDTH] / totals[:, SUBSPACE_WIDTH : SUBSPACE_WIDTH + 1]).astype(
        jnp.bfloat16
    )
    back = lax.all_to_all(merged, GROUP, split_axis=0, concat_axis=1, tiled=True)
    node_heads = back.reshape(block_len, members, SUBSPACE_WIDTH)[:, jnp.array(member_of)]
    node_heads = node_heads.reshape(block_len, -1)
    attended = jnp.dot(node_heads, final_projector, preferred_element_type=jnp.float32)
    normed = (
        attended
        * lax.rsqrt(jnp.mean(attended * attended, axis=-1, keepdims=True) + norm_eps)
        * mixing_layer_gain
    )
    return (vertex_embeddings.astype(jnp.float32) + local_term + normed).astype(jnp.bfloat16)


def solution(mesh):
    n_dom, n_head = mesh.shape["dom"], mesh.shape["head"]
    fine = Mesh(mesh.devices.reshape(n_dom // 2, 2, n_head), (PLANE, PAIR, "head"))
    in_specs = (
        P((PLANE, PAIR, "head"), None),
        P(DOM, "head", None),
        P(),
        P(),
        P(),
        P(),
        P(),
        P(),
        P(),
        P(),
        P(),
    )
    out_specs = P((PLANE, PAIR, "head"), None)
    return jax.shard_map(shards, mesh=fine, in_specs=in_specs, out_specs=out_specs, check_vma=False)
```

```python
import math

import jax
import jax.numpy as jnp
from jax import lax
from jax.sharding import Mesh
from jax.sharding import PartitionSpec as P

NUM_SUBSPACES = 8
SUBSPACE_WIDTH = 64
KEY_BLOCK = 2048

norm_eps = 1e-06

ROW = "x"
COLUMN = "z"
PAIR = "yhi"
DOM = (ROW, COLUMN, PAIR)
GROUP = (PAIR, "head")


def extended(shard, width):
    devices = lax.axis_size(ROW) * lax.axis_size(COLUMN) * lax.axis_size(PAIR)
    length = shard.shape[0]
    up = [(i, (i + 1) % devices) for i in range(devices - 1)]
    down = [(j, i) for i, j in up]
    last = lax.slice_in_dim(shard, length - width, length, axis=0)
    first = lax.slice_in_dim(shard, 0, width, axis=0)
    before = lax.ppermute(last, DOM, up)
    after = lax.ppermute(first, DOM, down)
    return jnp.concatenate([before, shard, after], axis=0)


def head_norm(projected, scales):
    rows = projected.shape[0]
    grouped = projected.reshape(rows, -1, SUBSPACE_WIDTH)
    mean_square = jnp.mean(grouped * grouped, axis=-1, keepdims=True)
    scaled = grouped * lax.rsqrt(mean_square + norm_eps)
    if scales is not None:
        scaled = scaled * scales[None, :, None]
    return scaled.reshape(rows, -1).astype(jnp.bfloat16)


def shards(
    vertex_embeddings,
    adjacent_group_bank_ids,
    coupling_strength_panels,
    asking_projector,
    lookup_projector,
    content_projector,
    final_projector,
    passing_inner_coefficients,
    passing_outer_coefficients,
    softness_per_subspace,
    mixing_layer_gain,
):
    block_len = vertex_embeddings.shape[0]
    group_size = lax.axis_size("head")
    pair_size = lax.axis_size(PAIR)
    members = group_size * pair_size
    slot_ids = adjacent_group_bank_ids.reshape(-1)
    halo_rows = extended(vertex_embeddings, block_len)
    me = lax.axis_index("head")
    gathered = [halo_rows]
    for shift in range(1, group_size):
        pairs = [(i, (i + shift) % group_size) for i in range(group_size)]
        gathered.append(lax.ppermute(halo_rows, "head", pairs))
    stacked = jnp.stack(gathered)
    order = (me - jnp.arange(group_size)) % group_size
    nearby = jnp.zeros_like(stacked).at[order].set(stacked).reshape(-1, halo_rows.shape[1])
    slot_order = slot_ids.reshape(3, group_size).T.reshape(-1)
    asking_vector_multiplier = softness_per_subspace / math.sqrt(SUBSPACE_WIDTH)
    queries = head_norm(
        jnp.dot(vertex_embeddings, asking_projector, preferred_element_type=jnp.float32),
        asking_vector_multiplier,
    )
    keys_all = head_norm(
        jnp.dot(vertex_embeddings, lookup_projector, preferred_element_type=jnp.float32), None
    )
    values_all = jnp.dot(
        vertex_embeddings, content_projector, preferred_element_type=jnp.float32
    ).astype(jnp.bfloat16)

    head_of = [(j % group_size) * pair_size + j // group_size for j in range(members)]
    member_of = [head_of.index(h) for h in range(NUM_SUBSPACES)]
    packed = jnp.stack(
        [t.reshape(block_len, NUM_SUBSPACES, SUBSPACE_WIDTH) for t in (queries, keys_all, values_all)],
        axis=2,
    )[:, jnp.array(head_of)]
    packed = packed.reshape(block_len, -1)
    mine = lax.all_to_all(packed, GROUP, split_axis=1, concat_axis=0, tiled=True)
    query_rows = mine.shape[0]
    head_queries = mine[:, :SUBSPACE_WIDTH]
    key_values = mine[:, SUBSPACE_WIDTH:]

    selected = jnp.take(coupling_strength_panels, jnp.maximum(slot_order, 0), axis=0)
    selected = jnp.where((slot_order >= 0)[:, None, None], selected, jnp.zeros_like(selected))
    wide_tiles = jnp.transpose(selected, (1, 0, 2)).reshape(block_len, -1)
    aggregate = jnp.dot(wide_tiles, nearby, preferred_element_type=jnp.float32).astype(jnp.bfloat16)
    hidden = jax.nn.gelu(
        jnp.dot(aggregate, passing_inner_coefficients, preferred_element_type=jnp.float32)
    ).astype(jnp.bfloat16)
    local_term = jnp.dot(hidden, passing_outer_coefficients, preferred_element_type=jnp.float32)

    local_term, head_queries = lax.optimization_barrier((local_term, head_queries))
    kv_in = lax.all_gather(key_values, COLUMN, axis=0, tiled=True)
    kv_in = lax.all_gather(kv_in, ROW, axis=0, tiled=True)
    key_count = kv_in.shape[0]
    block_step = min(KEY_BLOCK, key_count)
    ones = jnp.ones((block_step, SUBSPACE_WIDTH), jnp.bfloat16)

    def accumulate(turn_index, totals):
        block = lax.dynamic_slice_in_dim(kv_in, turn_index * block_step, block_step, 0)
        scores = jnp.einsum(
            "qd,kd->qk",
            head_queries,
            block[:, :SUBSPACE_WIDTH],
            preferred_element_type=jnp.float32,
        )
        weights = jnp.exp(scores).astype(jnp.bfloat16)
        widened = jnp.concatenate([block[:, SUBSPACE_WIDTH:], ones], axis=1)
        return totals + jnp.dot(weights, widened, preferred_element_type=jnp.float32)

    totals = lax.fori_loop(
        0,
        key_count // block_step,
        accumulate,
        jnp.zeros((query_rows, 2 * SUBSPACE_WIDTH), jnp.float32),
    )
    merged = (totals[:, :SUBSPACE_WIDTH] / totals[:, SUBSPACE_WIDTH : SUBSPACE_WIDTH + 1]).astype(
        jnp.bfloat16
    )
    back = lax.all_to_all(merged, GROUP, split_axis=0, concat_axis=1, tiled=True)
    node_heads = back.reshape(block_len, members, SUBSPACE_WIDTH)[:, jnp.array(member_of)]
    node_heads = node_heads.reshape(block_len, -1)
    attended = jnp.dot(node_heads, final_projector, preferred_element_type=jnp.float32)
    normed = (
        attended
        * lax.rsqrt(jnp.mean(attended * attended, axis=-1, keepdims=True) + norm_eps)
        * mixing_layer_gain
    )
    return (vertex_embeddings.astype(jnp.float32) + local_term + normed).astype(jnp.bfloat16)


def solution(mesh):
    n_dom, n_head = mesh.shape["dom"], mesh.shape["head"]
    fine = Mesh(mesh.devices.reshape(n_dom // 16, 8, 2, n_head), (ROW, COLUMN, PAIR, "head"))
    in_specs = (
        P((ROW, COLUMN, PAIR, "head"), None),
        P(DOM, "head", None),
        P(),
        P(),
        P(),
        P(),
        P(),
        P(),
        P(),
        P(),
        P(),
    )
    out_specs = P((ROW, COLUMN, PAIR, "head"), None)
    return jax.shard_map(shards, mesh=fine, in_specs=in_specs, out_specs=out_specs, check_vma=False)
```

```python
import math

import jax
import jax.numpy as jnp
from jax import lax
from jax.sharding import Mesh
from jax.sharding import PartitionSpec as P

NUM_SUBSPACES = 8
SUBSPACE_WIDTH = 64
KEY_BLOCK = 2048

norm_eps = 1e-06

ROW = "x"
COLUMN = "z"
PAIR = "yhi"
DOM = (ROW, COLUMN, PAIR)
GROUP = (PAIR, "head")


def extended(shard, width):
    devices = lax.axis_size(ROW) * lax.axis_size(COLUMN) * lax.axis_size(PAIR)
    length = shard.shape[0]
    up = [(i, (i + 1) % devices) for i in range(devices - 1)]
    down = [(j, i) for i, j in up]
    last = lax.slice_in_dim(shard, length - width, length, axis=0)
    first = lax.slice_in_dim(shard, 0, width, axis=0)
    before = lax.ppermute(last, DOM, up)
    after = lax.ppermute(first, DOM, down)
    return jnp.concatenate([before, shard, after], axis=0)


def head_norm(projected, scales):
    rows = projected.shape[0]
    grouped = projected.reshape(rows, -1, SUBSPACE_WIDTH)
    mean_square = jnp.mean(grouped * grouped, axis=-1, keepdims=True)
    scaled = grouped * lax.rsqrt(mean_square + norm_eps)
    if scales is not None:
        scaled = scaled * scales[None, :, None]
    return scaled.reshape(rows, -1).astype(jnp.bfloat16)


def shards(
    vertex_embeddings,
    adjacent_group_bank_ids,
    coupling_strength_panels,
    asking_projector,
    lookup_projector,
    content_projector,
    final_projector,
    passing_inner_coefficients,
    passing_outer_coefficients,
    softness_per_subspace,
    mixing_layer_gain,
):
    block_len = vertex_embeddings.shape[0]
    group_size = lax.axis_size("head")
    pair_size = lax.axis_size(PAIR)
    members = group_size * pair_size
    slot_ids = adjacent_group_bank_ids.reshape(-1)
    halo_rows = extended(vertex_embeddings, block_len)
    me = lax.axis_index("head")
    gathered = [halo_rows]
    for shift in range(1, group_size):
        pairs = [(i, (i + shift) % group_size) for i in range(group_size)]
        gathered.append(lax.ppermute(halo_rows, "head", pairs))
    stacked = jnp.stack(gathered)
    order = (me - jnp.arange(group_size)) % group_size
    nearby = jnp.zeros_like(stacked).at[order].set(stacked).reshape(-1, halo_rows.shape[1])
    slot_order = slot_ids.reshape(3, group_size).T.reshape(-1)
    asking_vector_multiplier = softness_per_subspace / math.sqrt(SUBSPACE_WIDTH)
    queries = head_norm(
        jnp.dot(vertex_embeddings, asking_projector, preferred_element_type=jnp.float32),
        asking_vector_multiplier,
    )
    keys_all = head_norm(
        jnp.dot(vertex_embeddings, lookup_projector, preferred_element_type=jnp.float32), None
    )
    values_all = jnp.dot(
        vertex_embeddings, content_projector, preferred_element_type=jnp.float32
    ).astype(jnp.bfloat16)

    head_of = [(j % group_size) * pair_size + j // group_size for j in range(members)]
    member_of = [head_of.index(h) for h in range(NUM_SUBSPACES)]
    packed = jnp.stack(
        [t.reshape(block_len, NUM_SUBSPACES, SUBSPACE_WIDTH) for t in (queries, keys_all, values_all)],
        axis=2,
    )[:, jnp.array(head_of)]
    packed = packed.reshape(block_len, -1)
    mine = lax.all_to_all(packed, GROUP, split_axis=1, concat_axis=0, tiled=True)
    query_rows = mine.shape[0]
    head_queries = mine[:, :SUBSPACE_WIDTH]
    key_values = mine[:, SUBSPACE_WIDTH:]

    selected = jnp.take(coupling_strength_panels, jnp.maximum(slot_order, 0), axis=0)
    selected = jnp.where((slot_order >= 0)[:, None, None], selected, jnp.zeros_like(selected))
    wide_tiles = jnp.transpose(selected, (1, 0, 2)).reshape(block_len, -1)
    aggregate = jnp.dot(wide_tiles, nearby, preferred_element_type=jnp.float32).astype(jnp.bfloat16)
    hidden = jax.nn.gelu(
        jnp.dot(aggregate, passing_inner_coefficients, preferred_element_type=jnp.float32)
    ).astype(jnp.bfloat16)
    local_term = jnp.dot(hidden, passing_outer_coefficients, preferred_element_type=jnp.float32)

    local_term, head_queries = lax.optimization_barrier((local_term, head_queries))
    kv_in = lax.all_gather(key_values, (ROW, COLUMN), axis=0, tiled=True)
    key_count = kv_in.shape[0]
    block_step = min(KEY_BLOCK, key_count)
    ones = jnp.ones((block_step, SUBSPACE_WIDTH), jnp.bfloat16)

    def accumulate(turn_index, totals):
        block = lax.dynamic_slice_in_dim(kv_in, turn_index * block_step, block_step, 0)
        scores = jnp.einsum(
            "qd,kd->qk",
            head_queries,
            block[:, :SUBSPACE_WIDTH],
            preferred_element_type=jnp.float32,
        )
        weights = jnp.exp(scores).astype(jnp.bfloat16)
        widened = jnp.concatenate([block[:, SUBSPACE_WIDTH:], ones], axis=1)
        return totals + jnp.dot(weights, widened, preferred_element_type=jnp.float32)

    totals = lax.fori_loop(
        0,
        key_count // block_step,
        accumulate,
        jnp.zeros((query_rows, 2 * SUBSPACE_WIDTH), jnp.float32),
    )
    merged = (totals[:, :SUBSPACE_WIDTH] / totals[:, SUBSPACE_WIDTH : SUBSPACE_WIDTH + 1]).astype(
        jnp.bfloat16
    )
    back = lax.all_to_all(merged, GROUP, split_axis=0, concat_axis=1, tiled=True)
    node_heads = back.reshape(block_len, members, SUBSPACE_WIDTH)[:, jnp.array(member_of)]
    node_heads = node_heads.reshape(block_len, -1)
    attended = jnp.dot(node_heads, final_projector, preferred_element_type=jnp.float32)
    normed = (
        attended
        * lax.rsqrt(jnp.mean(attended * attended, axis=-1, keepdims=True) + norm_eps)
        * mixing_layer_gain
    )
    return (vertex_embeddings.astype(jnp.float32) + local_term + normed).astype(jnp.bfloat16)


def solution(mesh):
    n_dom, n_head = mesh.shape["dom"], mesh.shape["head"]
    fine = Mesh(mesh.devices.reshape(n_dom // 16, 8, 2, n_head), (ROW, COLUMN, PAIR, "head"))
    in_specs = (
        P((ROW, COLUMN, PAIR, "head"), None),
        P(DOM, "head", None),
        P(),
        P(),
        P(),
        P(),
        P(),
        P(),
        P(),
        P(),
        P(),
    )
    out_specs = P((ROW, COLUMN, PAIR, "head"), None)
    return jax.shard_map(shards, mesh=fine, in_specs=in_specs, out_specs=out_specs, check_vma=False)
```

```python
import math

import jax
from jax.experimental import pallas as pl
from jax.experimental.pallas import tpu as pltpu
import jax.numpy as jnp
from jax import lax
from jax.sharding import Mesh
from jax.sharding import PartitionSpec as P

NUM_SUBSPACES = 8
SUBSPACE_WIDTH = 64
KEY_BLOCK = 8192
KEY_STEP = 2048
QUERY_STEP = 1024

norm_eps = 1e-06

ROW = "x"
COLUMN = "z"
PAIR = "yhi"
DOM = (ROW, COLUMN, PAIR)
GROUP = (PAIR, "head")


def extended(shard, width):
    devices = lax.axis_size(ROW) * lax.axis_size(COLUMN) * lax.axis_size(PAIR)
    length = shard.shape[0]
    up = [(i, (i + 1) % devices) for i in range(devices - 1)]
    down = [(j, i) for i, j in up]
    last = lax.slice_in_dim(shard, length - width, length, axis=0)
    first = lax.slice_in_dim(shard, 0, width, axis=0)
    before = lax.ppermute(last, DOM, up)
    after = lax.ppermute(first, DOM, down)
    return jnp.concatenate([before, shard, after], axis=0)


def head_norm(projected, scales):
    rows = projected.shape[0]
    grouped = projected.reshape(rows, -1, SUBSPACE_WIDTH)
    mean_square = jnp.mean(grouped * grouped, axis=-1, keepdims=True)
    scaled = grouped * lax.rsqrt(mean_square + norm_eps)
    if scales is not None:
        scaled = scaled * scales[None, :, None]
    return scaled.reshape(rows, -1).astype(jnp.bfloat16)


def attention_kernel(q_ref, kv_ref, o_ref):
    @pl.when(pl.program_id(0) == 0)
    def _():
        o_ref[...] = jnp.zeros_like(o_ref)

    q_step = min(QUERY_STEP, q_ref.shape[0])
    k_step = min(KEY_STEP, kv_ref.shape[0])
    q_count = q_ref.shape[0] // q_step
    k_count = kv_ref.shape[0] // k_step

    def body(turn, carry):
        rows = pl.ds(pl.multiple_of((turn // k_count) * q_step, q_step), q_step)
        keys = pl.ds(pl.multiple_of((turn % k_count) * k_step, k_step), k_step)
        block = kv_ref[keys, :]
        scores = lax.dot_general(
            q_ref[rows, :], block, (((1,), (1,)), ((), ())), preferred_element_type=jnp.float32
        )
        weights = jnp.exp(scores).astype(jnp.bfloat16)
        lane = lax.broadcasted_iota(jnp.int32, block.shape, 1)
        widened = jnp.where(lane < SUBSPACE_WIDTH, jnp.ones_like(block), block)
        o_ref[rows, :] += jnp.dot(weights, widened, preferred_element_type=jnp.float32)
        return carry

    lax.fori_loop(0, q_count * k_count, body, 0)


def attend(padded_queries, key_values):
    rows, width = padded_queries.shape
    keys = key_values.shape[0]
    block = min(KEY_BLOCK, keys)
    flops = 4 * rows * keys * width
    return pl.pallas_call(
        attention_kernel,
        grid=(keys // block,),
        in_specs=[
            pl.BlockSpec((rows, width), lambda j: (0, 0)),
            pl.BlockSpec((block, width), lambda j: (j, 0)),
        ],
        out_specs=pl.BlockSpec((rows, width), lambda j: (0, 0)),
        out_shape=jax.ShapeDtypeStruct((rows, width), jnp.float32),
        compiler_params=pltpu.CompilerParams(dimension_semantics=("arbitrary",)),
        cost_estimate=pl.CostEstimate(
            flops=flops, transcendentals=rows * keys, bytes_accessed=2 * keys * width + 6 * rows * width
        ),
    )(padded_queries, key_values)


def shards(
    vertex_embeddings,
    adjacent_group_bank_ids,
    coupling_strength_panels,
    asking_projector,
    lookup_projector,
    content_projector,
    final_projector,
    passing_inner_coefficients,
    passing_outer_coefficients,
    softness_per_subspace,
    mixing_layer_gain,
):
    block_len = vertex_embeddings.shape[0]
    group_size = lax.axis_size("head")
    pair_size = lax.axis_size(PAIR)
    members = group_size * pair_size
    slot_ids = adjacent_group_bank_ids.reshape(-1)
    halo_rows = extended(vertex_embeddings, block_len)
    me = lax.axis_index("head")
    gathered = [halo_rows]
    for shift in range(1, group_size):
        pairs = [(i, (i + shift) % group_size) for i in range(group_size)]
        gathered.append(lax.ppermute(halo_rows, "head", pairs))
    stacked = jnp.stack(gathered)
    order = (me - jnp.arange(group_size)) % group_size
    nearby = jnp.zeros_like(stacked).at[order].set(stacked).reshape(-1, halo_rows.shape[1])
    slot_order = slot_ids.reshape(3, group_size).T.reshape(-1)
    asking_vector_multiplier = softness_per_subspace / math.sqrt(SUBSPACE_WIDTH)
    queries = head_norm(
        jnp.dot(vertex_embeddings, asking_projector, preferred_element_type=jnp.float32),
        asking_vector_multiplier,
    )
    keys_all = head_norm(
        jnp.dot(vertex_embeddings, lookup_projector, preferred_element_type=jnp.float32), None
    )
    values_all = jnp.dot(
        vertex_embeddings, content_projector, preferred_element_type=jnp.float32
    ).astype(jnp.bfloat16)

    head_of = [(j % group_size) * pair_size + j // group_size for j in range(members)]
    member_of = [head_of.index(h) for h in range(NUM_SUBSPACES)]
    packed = jnp.stack(
        [t.reshape(block_len, NUM_SUBSPACES, SUBSPACE_WIDTH) for t in (queries, keys_all, values_all)],
        axis=2,
    )[:, jnp.array(head_of)]
    packed = packed.reshape(block_len, -1)
    mine = lax.all_to_all(packed, GROUP, split_axis=1, concat_axis=0, tiled=True)
    query_rows = mine.shape[0]
    head_queries = mine[:, :SUBSPACE_WIDTH]
    key_values = mine[:, SUBSPACE_WIDTH:]

    selected = jnp.take(coupling_strength_panels, jnp.maximum(slot_order, 0), axis=0)
    selected = jnp.where((slot_order >= 0)[:, None, None], selected, jnp.zeros_like(selected))
    wide_tiles = jnp.transpose(selected, (1, 0, 2)).reshape(block_len, -1)
    aggregate = jnp.dot(wide_tiles, nearby, preferred_element_type=jnp.float32).astype(jnp.bfloat16)
    hidden = jax.nn.gelu(
        jnp.dot(aggregate, passing_inner_coefficients, preferred_element_type=jnp.float32)
    ).astype(jnp.bfloat16)
    local_term = jnp.dot(hidden, passing_outer_coefficients, preferred_element_type=jnp.float32)

    local_term, head_queries = lax.optimization_barrier((local_term, head_queries))
    kv_in = lax.all_gather(key_values, (ROW, COLUMN), axis=0, tiled=True)
    padded_queries = jnp.concatenate([head_queries, jnp.zeros_like(head_queries)], axis=1)
    totals = attend(padded_queries, kv_in)
    merged = (totals[:, SUBSPACE_WIDTH:] / totals[:, :1]).astype(jnp.bfloat16)
    back = lax.all_to_all(merged, GROUP, split_axis=0, concat_axis=1, tiled=True)
    node_heads = back.reshape(block_len, members, SUBSPACE_WIDTH)[:, jnp.array(member_of)]
    node_heads = node_heads.reshape(block_len, -1)
    attended = jnp.dot(node_heads, final_projector, preferred_element_type=jnp.float32)
    normed = (
        attended
        * lax.rsqrt(jnp.mean(attended * attended, axis=-1, keepdims=True) + norm_eps)
        * mixing_layer_gain
    )
    return (vertex_embeddings.astype(jnp.float32) + local_term + normed).astype(jnp.bfloat16)


def solution(mesh):
    n_dom, n_head = mesh.shape["dom"], mesh.shape["head"]
    fine = Mesh(mesh.devices.reshape(n_dom // 16, 8, 2, n_head), (ROW, COLUMN, PAIR, "head"))
    in_specs = (
        P((ROW, COLUMN, PAIR, "head"), None),
        P(DOM, "head", None),
        P(),
        P(),
        P(),
        P(),
        P(),
        P(),
        P(),
        P(),
        P(),
    )
    out_specs = P((ROW, COLUMN, PAIR, "head"), None)
    return jax.shard_map(shards, mesh=fine, in_specs=in_specs, out_specs=out_specs, check_vma=False)
```

```python
import math

import jax
from jax.experimental import pallas as pl
from jax.experimental.pallas import tpu as pltpu
import jax.numpy as jnp
from jax import lax
from jax.sharding import Mesh
from jax.sharding import PartitionSpec as P

NUM_SUBSPACES = 8
SUBSPACE_WIDTH = 64

norm_eps = 1e-06

ROW = "x"
COLUMN = "z"
PAIR = "yhi"
DOM = (ROW, COLUMN, PAIR)
GROUP = (PAIR, "head")


def extended(shard, width):
    devices = lax.axis_size(ROW) * lax.axis_size(COLUMN) * lax.axis_size(PAIR)
    length = shard.shape[0]
    up = [(i, (i + 1) % devices) for i in range(devices - 1)]
    down = [(j, i) for i, j in up]
    last = lax.slice_in_dim(shard, length - width, length, axis=0)
    first = lax.slice_in_dim(shard, 0, width, axis=0)
    before = lax.ppermute(last, DOM, up)
    after = lax.ppermute(first, DOM, down)
    return jnp.concatenate([before, shard, after], axis=0)


def head_norm(projected, scales):
    rows = projected.shape[0]
    grouped = projected.reshape(rows, -1, SUBSPACE_WIDTH)
    mean_square = jnp.mean(grouped * grouped, axis=-1, keepdims=True)
    scaled = grouped * lax.rsqrt(mean_square + norm_eps)
    if scales is not None:
        scaled = scaled * scales[None, :, None]
    return scaled.reshape(rows, -1).astype(jnp.bfloat16)


def accumulate(q_ref, block, o_ref):
    scores = lax.dot_general(
        q_ref[...], block, (((1,), (1,)), ((), ())), preferred_element_type=jnp.float32
    )
    weights = jnp.exp(scores).astype(jnp.bfloat16)
    lane = lax.broadcasted_iota(jnp.int32, block.shape, 1)
    widened = jnp.where(lane < SUBSPACE_WIDTH, jnp.ones_like(block), block)
    o_ref[...] += jnp.dot(weights, widened, preferred_element_type=jnp.float32)


def gathering_kernel(q_ref, kv_ref, o_ref, slots, send_sem, recv_sem):
    columns = lax.axis_size(COLUMN)
    positions = lax.axis_size(ROW) * columns
    me = lax.axis_index(ROW) * columns + lax.axis_index(COLUMN)
    pair = lax.axis_index(PAIR)
    member = lax.axis_index("head")

    def copy_with(offset):
        target = lax.rem(me + offset, positions)
        return pltpu.make_async_remote_copy(
            src_ref=kv_ref,
            dst_ref=slots.at[me],
            send_sem=send_sem.at[offset],
            recv_sem=recv_sem.at[me],
            device_id=(target // columns, lax.rem(target, columns), pair, member),
            device_id_type=pl.DeviceIdType.MESH,
        )

    def arrival_from(offset):
        source = lax.rem(me - offset + positions, positions)
        return source, pltpu.make_async_remote_copy(
            src_ref=kv_ref,
            dst_ref=slots.at[source],
            send_sem=send_sem.at[offset],
            recv_sem=recv_sem.at[source],
            device_id=(source // columns, lax.rem(source, columns), pair, member),
            device_id_type=pl.DeviceIdType.MESH,
        )

    def send(offset, carry):
        copy_with(offset).start()
        return carry

    lax.fori_loop(1, positions, send, 0)
    o_ref[...] = jnp.zeros_like(o_ref)
    accumulate(q_ref, kv_ref[...], o_ref)

    def receive(offset, carry):
        source, arrival = arrival_from(offset)
        arrival.wait_recv()
        accumulate(q_ref, slots[source], o_ref)
        return carry

    lax.fori_loop(1, positions, receive, 0)

    def finish(offset, carry):
        copy_with(offset).wait_send()
        return carry

    lax.fori_loop(1, positions, finish, 0)


def gather_attend(padded_queries, key_values):
    rows, width = padded_queries.shape
    positions = lax.axis_size(ROW) * lax.axis_size(COLUMN)
    keys = positions * key_values.shape[0]
    return pl.pallas_call(
        gathering_kernel,
        in_specs=[pl.BlockSpec(memory_space=pltpu.VMEM)] * 2,
        out_specs=pl.BlockSpec(memory_space=pltpu.VMEM),
        out_shape=jax.ShapeDtypeStruct((rows, width), jnp.float32),
        scratch_shapes=[
            pltpu.VMEM((positions,) + key_values.shape, key_values.dtype),
            pltpu.SemaphoreType.DMA((positions,)),
            pltpu.SemaphoreType.DMA((positions,)),
        ],
        compiler_params=pltpu.CompilerParams(has_side_effects=True),
        cost_estimate=pl.CostEstimate(
            flops=4 * rows * keys * width,
            transcendentals=rows * keys,
            bytes_accessed=2 * keys * width + 6 * rows * width,
        ),
    )(padded_queries, key_values)


def shards(
    vertex_embeddings,
    adjacent_group_bank_ids,
    coupling_strength_panels,
    asking_projector,
    lookup_projector,
    content_projector,
    final_projector,
    passing_inner_coefficients,
    passing_outer_coefficients,
    softness_per_subspace,
    mixing_layer_gain,
):
    block_len = vertex_embeddings.shape[0]
    group_size = lax.axis_size("head")
    pair_size = lax.axis_size(PAIR)
    members = group_size * pair_size
    slot_ids = adjacent_group_bank_ids.reshape(-1)
    halo_rows = extended(vertex_embeddings, block_len)
    me = lax.axis_index("head")
    gathered = [halo_rows]
    for shift in range(1, group_size):
        pairs = [(i, (i + shift) % group_size) for i in range(group_size)]
        gathered.append(lax.ppermute(halo_rows, "head", pairs))
    stacked = jnp.stack(gathered)
    order = (me - jnp.arange(group_size)) % group_size
    nearby = jnp.zeros_like(stacked).at[order].set(stacked).reshape(-1, halo_rows.shape[1])
    slot_order = slot_ids.reshape(3, group_size).T.reshape(-1)
    asking_vector_multiplier = softness_per_subspace / math.sqrt(SUBSPACE_WIDTH)
    queries = head_norm(
        jnp.dot(vertex_embeddings, asking_projector, preferred_element_type=jnp.float32),
        asking_vector_multiplier,
    )
    keys_all = head_norm(
        jnp.dot(vertex_embeddings, lookup_projector, preferred_element_type=jnp.float32), None
    )
    values_all = jnp.dot(
        vertex_embeddings, content_projector, preferred_element_type=jnp.float32
    ).astype(jnp.bfloat16)

    head_of = [(j % group_size) * pair_size + j // group_size for j in range(members)]
    member_of = [head_of.index(h) for h in range(NUM_SUBSPACES)]
    packed = jnp.stack(
        [t.reshape(block_len, NUM_SUBSPACES, SUBSPACE_WIDTH) for t in (queries, keys_all, values_all)],
        axis=2,
    )[:, jnp.array(head_of)]
    packed = packed.reshape(block_len, -1)
    mine = lax.all_to_all(packed, GROUP, split_axis=1, concat_axis=0, tiled=True)
    query_rows = mine.shape[0]
    head_queries = mine[:, :SUBSPACE_WIDTH]
    key_values = mine[:, SUBSPACE_WIDTH:]

    selected = jnp.take(coupling_strength_panels, jnp.maximum(slot_order, 0), axis=0)
    selected = jnp.where((slot_order >= 0)[:, None, None], selected, jnp.zeros_like(selected))
    wide_tiles = jnp.transpose(selected, (1, 0, 2)).reshape(block_len, -1)
    aggregate = jnp.dot(wide_tiles, nearby, preferred_element_type=jnp.float32).astype(jnp.bfloat16)
    hidden = jax.nn.gelu(
        jnp.dot(aggregate, passing_inner_coefficients, preferred_element_type=jnp.float32)
    ).astype(jnp.bfloat16)
    local_term = jnp.dot(hidden, passing_outer_coefficients, preferred_element_type=jnp.float32)

    local_term, head_queries = lax.optimization_barrier((local_term, head_queries))
    padded_queries = jnp.concatenate([head_queries, jnp.zeros_like(head_queries)], axis=1)
    totals = gather_attend(padded_queries, key_values)
    merged = (totals[:, SUBSPACE_WIDTH:] / totals[:, :1]).astype(jnp.bfloat16)
    back = lax.all_to_all(merged, GROUP, split_axis=0, concat_axis=1, tiled=True)
    node_heads = back.reshape(block_len, members, SUBSPACE_WIDTH)[:, jnp.array(member_of)]
    node_heads = node_heads.reshape(block_len, -1)
    attended = jnp.dot(node_heads, final_projector, preferred_element_type=jnp.float32)
    normed = (
        attended
        * lax.rsqrt(jnp.mean(attended * attended, axis=-1, keepdims=True) + norm_eps)
        * mixing_layer_gain
    )
    return (vertex_embeddings.astype(jnp.float32) + local_term + normed).astype(jnp.bfloat16)


def solution(mesh):
    n_dom, n_head = mesh.shape["dom"], mesh.shape["head"]
    fine = Mesh(mesh.devices.reshape(n_dom // 16, 8, 2, n_head), (ROW, COLUMN, PAIR, "head"))
    in_specs = (
        P((ROW, COLUMN, PAIR, "head"), None),
        P(DOM, "head", None),
        P(),
        P(),
        P(),
        P(),
        P(),
        P(),
        P(),
        P(),
        P(),
    )
    out_specs = P((ROW, COLUMN, PAIR, "head"), None)
    return jax.shard_map(shards, mesh=fine, in_specs=in_specs, out_specs=out_specs, check_vma=False)
```

```python
import math

import jax
from jax.experimental import pallas as pl
from jax.experimental.pallas import tpu as pltpu
import jax.numpy as jnp
from jax import lax
from jax.sharding import Mesh
from jax.sharding import PartitionSpec as P

NUM_SUBSPACES = 8
SUBSPACE_WIDTH = 64
KEY_BLOCK = 8192
KEY_STEP = 2048
QUERY_STEP = 1024

norm_eps = 1e-06

ROW = "xhi"
NEIGHBOUR = "xlo"
COLUMN = "z"
PAIR = "yhi"
DOM = (ROW, NEIGHBOUR, COLUMN, PAIR)
GROUP = (PAIR, "head")


def extended(shard, width):
    devices = lax.axis_size(ROW) * lax.axis_size(NEIGHBOUR) * lax.axis_size(COLUMN) * lax.axis_size(PAIR)
    length = shard.shape[0]
    up = [(i, (i + 1) % devices) for i in range(devices - 1)]
    down = [(j, i) for i, j in up]
    last = lax.slice_in_dim(shard, length - width, length, axis=0)
    first = lax.slice_in_dim(shard, 0, width, axis=0)
    before = lax.ppermute(last, DOM, up)
    after = lax.ppermute(first, DOM, down)
    return jnp.concatenate([before, shard, after], axis=0)


def head_norm(projected, scales):
    rows = projected.shape[0]
    grouped = projected.reshape(rows, -1, SUBSPACE_WIDTH)
    mean_square = jnp.mean(grouped * grouped, axis=-1, keepdims=True)
    scaled = grouped * lax.rsqrt(mean_square + norm_eps)
    if scales is not None:
        scaled = scaled * scales[None, :, None]
    return scaled.reshape(rows, -1).astype(jnp.bfloat16)


def attention_kernel(q_ref, kv_ref, o_ref):
    @pl.when(pl.program_id(0) == 0)
    def _():
        o_ref[...] = jnp.zeros_like(o_ref)

    q_step = min(QUERY_STEP, q_ref.shape[0])
    k_step = min(KEY_STEP, kv_ref.shape[0])
    q_count = q_ref.shape[0] // q_step
    k_count = kv_ref.shape[0] // k_step

    def body(turn, carry):
        rows = pl.ds(pl.multiple_of((turn // k_count) * q_step, q_step), q_step)
        keys = pl.ds(pl.multiple_of((turn % k_count) * k_step, k_step), k_step)
        block = kv_ref[keys, :]
        scores = lax.dot_general(
            q_ref[rows, :], block, (((1,), (1,)), ((), ())), preferred_element_type=jnp.float32
        )
        weights = jnp.exp(scores).astype(jnp.bfloat16)
        lane = lax.broadcasted_iota(jnp.int32, block.shape, 1)
        widened = jnp.where(lane < SUBSPACE_WIDTH, jnp.ones_like(block), block)
        o_ref[rows, :] += jnp.dot(weights, widened, preferred_element_type=jnp.float32)
        return carry

    lax.fori_loop(0, q_count * k_count, body, 0)


def attend(padded_queries, key_values):
    rows, width = padded_queries.shape
    keys = key_values.shape[0]
    block = min(KEY_BLOCK, keys)
    flops = 4 * rows * keys * width
    return pl.pallas_call(
        attention_kernel,
        grid=(keys // block,),
        in_specs=[
            pl.BlockSpec((rows, width), lambda j: (0, 0)),
            pl.BlockSpec((block, width), lambda j: (j, 0)),
        ],
        out_specs=pl.BlockSpec((rows, width), lambda j: (0, 0)),
        out_shape=jax.ShapeDtypeStruct((rows, width), jnp.float32),
        compiler_params=pltpu.CompilerParams(dimension_semantics=("arbitrary",)),
        cost_estimate=pl.CostEstimate(
            flops=flops, transcendentals=rows * keys, bytes_accessed=2 * keys * width + 6 * rows * width
        ),
    )(padded_queries, key_values)


def shards(
    vertex_embeddings,
    adjacent_group_bank_ids,
    coupling_strength_panels,
    asking_projector,
    lookup_projector,
    content_projector,
    final_projector,
    passing_inner_coefficients,
    passing_outer_coefficients,
    softness_per_subspace,
    mixing_layer_gain,
):
    block_len = vertex_embeddings.shape[0]
    group_size = lax.axis_size("head")
    pair_size = lax.axis_size(PAIR)
    members = group_size * pair_size
    slot_ids = adjacent_group_bank_ids.reshape(-1)
    halo_rows = extended(vertex_embeddings, block_len)
    me = lax.axis_index("head")
    gathered = [halo_rows]
    for shift in range(1, group_size):
        pairs = [(i, (i + shift) % group_size) for i in range(group_size)]
        gathered.append(lax.ppermute(halo_rows, "head", pairs))
    stacked = jnp.stack(gathered)
    order = (me - jnp.arange(group_size)) % group_size
    nearby = jnp.zeros_like(stacked).at[order].set(stacked).reshape(-1, halo_rows.shape[1])
    slot_order = slot_ids.reshape(3, group_size).T.reshape(-1)
    asking_vector_multiplier = softness_per_subspace / math.sqrt(SUBSPACE_WIDTH)
    queries = head_norm(
        jnp.dot(vertex_embeddings, asking_projector, preferred_element_type=jnp.float32),
        asking_vector_multiplier,
    )
    keys_all = head_norm(
        jnp.dot(vertex_embeddings, lookup_projector, preferred_element_type=jnp.float32), None
    )
    values_all = jnp.dot(
        vertex_embeddings, content_projector, preferred_element_type=jnp.float32
    ).astype(jnp.bfloat16)

    head_of = [(j % group_size) * pair_size + j // group_size for j in range(members)]
    member_of = [head_of.index(h) for h in range(NUM_SUBSPACES)]
    packed = jnp.stack(
        [t.reshape(block_len, NUM_SUBSPACES, SUBSPACE_WIDTH) for t in (queries, keys_all, values_all)],
        axis=2,
    )[:, jnp.array(head_of)]
    packed = packed.reshape(block_len, -1)
    mine = lax.all_to_all(packed, GROUP, split_axis=1, concat_axis=0, tiled=True)
    query_rows = mine.shape[0]
    head_queries = mine[:, :SUBSPACE_WIDTH]
    key_values = mine[:, SUBSPACE_WIDTH:]

    selected = jnp.take(coupling_strength_panels, jnp.maximum(slot_order, 0), axis=0)
    selected = jnp.where((slot_order >= 0)[:, None, None], selected, jnp.zeros_like(selected))
    wide_tiles = jnp.transpose(selected, (1, 0, 2)).reshape(block_len, -1)
    aggregate = jnp.dot(wide_tiles, nearby, preferred_element_type=jnp.float32).astype(jnp.bfloat16)
    hidden = jax.nn.gelu(
        jnp.dot(aggregate, passing_inner_coefficients, preferred_element_type=jnp.float32)
    ).astype(jnp.bfloat16)
    local_term = jnp.dot(hidden, passing_outer_coefficients, preferred_element_type=jnp.float32)

    local_term, head_queries = lax.optimization_barrier((local_term, head_queries))
    swap = [(0, 1), (1, 0)]
    pair_queries = jnp.concatenate(
        [head_queries, lax.ppermute(head_queries, NEIGHBOUR, swap)], axis=0
    )
    kv_in = lax.all_gather(key_values, (ROW, COLUMN), axis=0, tiled=True)
    padded_queries = jnp.concatenate([pair_queries, jnp.zeros_like(pair_queries)], axis=1)
    totals = attend(padded_queries, kv_in)
    totals = totals[:query_rows] + lax.ppermute(totals[query_rows:], NEIGHBOUR, swap)
    merged = (totals[:, SUBSPACE_WIDTH:] / totals[:, :1]).astype(jnp.bfloat16)
    back = lax.all_to_all(merged, GROUP, split_axis=0, concat_axis=1, tiled=True)
    node_heads = back.reshape(block_len, members, SUBSPACE_WIDTH)[:, jnp.array(member_of)]
    node_heads = node_heads.reshape(block_len, -1)
    attended = jnp.dot(node_heads, final_projector, preferred_element_type=jnp.float32)
    normed = (
        attended
        * lax.rsqrt(jnp.mean(attended * attended, axis=-1, keepdims=True) + norm_eps)
        * mixing_layer_gain
    )
    return (vertex_embeddings.astype(jnp.float32) + local_term + normed).astype(jnp.bfloat16)


def solution(mesh):
    n_dom, n_head = mesh.shape["dom"], mesh.shape["head"]
    fine = Mesh(
        mesh.devices.reshape(n_dom // 32, 2, 8, 2, n_head), (ROW, NEIGHBOUR, COLUMN, PAIR, "head")
    )
    in_specs = (
        P((ROW, NEIGHBOUR, COLUMN, PAIR, "head"), None),
        P(DOM, "head", None),
        P(),
        P(),
        P(),
        P(),
        P(),
        P(),
        P(),
        P(),
        P(),
    )
    out_specs = P((ROW, NEIGHBOUR, COLUMN, PAIR, "head"), None)
    return jax.shard_map(shards, mesh=fine, in_specs=in_specs, out_specs=out_specs, check_vma=False)
```

```python
import math

import jax
from jax.experimental import pallas as pl
from jax.experimental.pallas import tpu as pltpu
import jax.numpy as jnp
from jax import lax
from jax.sharding import Mesh
from jax.sharding import PartitionSpec as P

NUM_SUBSPACES = 8
SUBSPACE_WIDTH = 64
KEY_BLOCK = 8192
KEY_STEP = 2048
QUERY_STEP = 1024

norm_eps = 1e-06

ROW = "x"
COLUMN = "z"
PAIR = "yhi"
DOM = (ROW, COLUMN, PAIR)
GROUP = (PAIR, "head")


def extended(shard, width):
    devices = lax.axis_size(ROW) * lax.axis_size(COLUMN) * lax.axis_size(PAIR)
    length = shard.shape[0]
    up = [(i, (i + 1) % devices) for i in range(devices - 1)]
    down = [(j, i) for i, j in up]
    last = lax.slice_in_dim(shard, length - width, length, axis=0)
    first = lax.slice_in_dim(shard, 0, width, axis=0)
    before = lax.ppermute(last, DOM, up)
    after = lax.ppermute(first, DOM, down)
    return jnp.concatenate([before, shard, after], axis=0)


def head_norm(projected, scales):
    rows = projected.shape[0]
    grouped = projected.reshape(rows, -1, SUBSPACE_WIDTH)
    mean_square = jnp.mean(grouped * grouped, axis=-1, keepdims=True)
    scaled = grouped * lax.rsqrt(mean_square + norm_eps)
    if scales is not None:
        scaled = scaled * scales[None, :, None]
    return scaled.reshape(rows, -1).astype(jnp.bfloat16)


def attention_kernel(q_ref, kv_ref, o_ref):
    @pl.when(pl.program_id(0) == 0)
    def _():
        o_ref[...] = jnp.zeros_like(o_ref)

    q_step = min(QUERY_STEP, q_ref.shape[0])
    k_step = min(KEY_STEP, kv_ref.shape[0])
    q_count = q_ref.shape[0] // q_step
    k_count = kv_ref.shape[0] // k_step

    def body(turn, carry):
        rows = pl.ds(pl.multiple_of((turn // k_count) * q_step, q_step), q_step)
        keys = pl.ds(pl.multiple_of((turn % k_count) * k_step, k_step), k_step)
        block = kv_ref[keys, :]
        scores = lax.dot_general(
            q_ref[rows, :], block, (((1,), (1,)), ((), ())), preferred_element_type=jnp.float32
        )
        weights = jnp.exp(scores).astype(jnp.bfloat16)
        lane = lax.broadcasted_iota(jnp.int32, block.shape, 1)
        widened = jnp.where(lane < SUBSPACE_WIDTH, jnp.ones_like(block), block)
        o_ref[rows, :] += jnp.dot(weights, widened, preferred_element_type=jnp.float32)
        return carry

    lax.fori_loop(0, q_count * k_count, body, 0)


def attend(padded_queries, key_values):
    rows, width = padded_queries.shape
    keys = key_values.shape[0]
    block = min(KEY_BLOCK, keys)
    flops = 4 * rows * keys * width
    return pl.pallas_call(
        attention_kernel,
        grid=(keys // block,),
        in_specs=[
            pl.BlockSpec((rows, width), lambda j: (0, 0)),
            pl.BlockSpec((block, width), lambda j: (j, 0)),
        ],
        out_specs=pl.BlockSpec((rows, width), lambda j: (0, 0)),
        out_shape=jax.ShapeDtypeStruct((rows, width), jnp.float32),
        compiler_params=pltpu.CompilerParams(dimension_semantics=("arbitrary",)),
        cost_estimate=pl.CostEstimate(
            flops=flops, transcendentals=rows * keys, bytes_accessed=2 * keys * width + 6 * rows * width
        ),
    )(padded_queries, key_values)


def shards(
    vertex_embeddings,
    adjacent_group_bank_ids,
    coupling_strength_panels,
    asking_projector,
    lookup_projector,
    content_projector,
    final_projector,
    passing_inner_coefficients,
    passing_outer_coefficients,
    softness_per_subspace,
    mixing_layer_gain,
):
    block_len = vertex_embeddings.shape[0]
    group_size = lax.axis_size("head")
    pair_size = lax.axis_size(PAIR)
    members = group_size * pair_size
    slot_ids = adjacent_group_bank_ids.reshape(-1)
    halo_rows = extended(vertex_embeddings, block_len)
    me = lax.axis_index("head")
    gathered = [halo_rows]
    for shift in range(1, group_size):
        pairs = [(i, (i + shift) % group_size) for i in range(group_size)]
        gathered.append(lax.ppermute(halo_rows, "head", pairs))
    stacked = jnp.stack(gathered)
    order = (me - jnp.arange(group_size)) % group_size
    nearby = jnp.zeros_like(stacked).at[order].set(stacked).reshape(-1, halo_rows.shape[1])
    slot_order = slot_ids.reshape(3, group_size).T.reshape(-1)
    asking_vector_multiplier = softness_per_subspace / math.sqrt(SUBSPACE_WIDTH)
    keys_all = head_norm(
        jnp.dot(vertex_embeddings, lookup_projector, preferred_element_type=jnp.float32), None
    )
    values_all = jnp.dot(
        vertex_embeddings, content_projector, preferred_element_type=jnp.float32
    ).astype(jnp.bfloat16)

    head_of = [(j % group_size) * pair_size + j // group_size for j in range(members)]
    member_of = [head_of.index(h) for h in range(NUM_SUBSPACES)]

    def to_members(parts):
        packed = jnp.stack(
            [t.reshape(block_len, NUM_SUBSPACES, SUBSPACE_WIDTH) for t in parts], axis=2
        )[:, jnp.array(head_of)]
        return lax.all_to_all(
            packed.reshape(block_len, -1), GROUP, split_axis=1, concat_axis=0, tiled=True
        )

    key_values = to_members((keys_all, values_all))
    kv_in = lax.all_gather(key_values, (ROW, COLUMN), axis=0, tiled=True)
    queries = head_norm(
        jnp.dot(vertex_embeddings, asking_projector, preferred_element_type=jnp.float32),
        asking_vector_multiplier,
    )
    head_queries = to_members((queries,))
    query_rows = head_queries.shape[0]

    selected = jnp.take(coupling_strength_panels, jnp.maximum(slot_order, 0), axis=0)
    selected = jnp.where((slot_order >= 0)[:, None, None], selected, jnp.zeros_like(selected))
    wide_tiles = jnp.transpose(selected, (1, 0, 2)).reshape(block_len, -1)
    aggregate = jnp.dot(wide_tiles, nearby, preferred_element_type=jnp.float32).astype(jnp.bfloat16)
    hidden = jax.nn.gelu(
        jnp.dot(aggregate, passing_inner_coefficients, preferred_element_type=jnp.float32)
    ).astype(jnp.bfloat16)
    local_term = jnp.dot(hidden, passing_outer_coefficients, preferred_element_type=jnp.float32)

    local_term, head_queries = lax.optimization_barrier((local_term, head_queries))
    padded_queries = jnp.concatenate([head_queries, jnp.zeros_like(head_queries)], axis=1)
    totals = attend(padded_queries, kv_in)
    merged = (totals[:, SUBSPACE_WIDTH:] / totals[:, :1]).astype(jnp.bfloat16)
    back = lax.all_to_all(merged, GROUP, split_axis=0, concat_axis=1, tiled=True)
    node_heads = back.reshape(block_len, members, SUBSPACE_WIDTH)[:, jnp.array(member_of)]
    node_heads = node_heads.reshape(block_len, -1)
    attended = jnp.dot(node_heads, final_projector, preferred_element_type=jnp.float32)
    normed = (
        attended
        * lax.rsqrt(jnp.mean(attended * attended, axis=-1, keepdims=True) + norm_eps)
        * mixing_layer_gain
    )
    return (vertex_embeddings.astype(jnp.float32) + local_term + normed).astype(jnp.bfloat16)


def solution(mesh):
    n_dom, n_head = mesh.shape["dom"], mesh.shape["head"]
    fine = Mesh(mesh.devices.reshape(n_dom // 16, 8, 2, n_head), (ROW, COLUMN, PAIR, "head"))
    in_specs = (
        P((ROW, COLUMN, PAIR, "head"), None),
        P(DOM, "head", None),
        P(),
        P(),
        P(),
        P(),
        P(),
        P(),
        P(),
        P(),
        P(),
    )
    out_specs = P((ROW, COLUMN, PAIR, "head"), None)
    return jax.shard_map(shards, mesh=fine, in_specs=in_specs, out_specs=out_specs, check_vma=False)
```

```python
import math

import jax
from jax.experimental import pallas as pl
from jax.experimental.pallas import tpu as pltpu
import jax.numpy as jnp
from jax import lax
from jax.sharding import Mesh
from jax.sharding import PartitionSpec as P

NUM_SUBSPACES = 8
SUBSPACE_WIDTH = 64
KEY_BLOCK = 8192
KEY_STEP = 4096
QUERY_STEP = 1024

norm_eps = 1e-06

ROW = "x"
COLUMN = "z"
PAIR = "yhi"
DOM = (ROW, COLUMN, PAIR)
GROUP = (PAIR, "head")


def extended(shard, width):
    devices = lax.axis_size(ROW) * lax.axis_size(COLUMN) * lax.axis_size(PAIR)
    length = shard.shape[0]
    up = [(i, (i + 1) % devices) for i in range(devices - 1)]
    down = [(j, i) for i, j in up]
    last = lax.slice_in_dim(shard, length - width, length, axis=0)
    first = lax.slice_in_dim(shard, 0, width, axis=0)
    before = lax.ppermute(last, DOM, up)
    after = lax.ppermute(first, DOM, down)
    return jnp.concatenate([before, shard, after], axis=0)


def head_norm(projected, scales):
    rows = projected.shape[0]
    grouped = projected.reshape(rows, -1, SUBSPACE_WIDTH)
    mean_square = jnp.mean(grouped * grouped, axis=-1, keepdims=True)
    scaled = grouped * lax.rsqrt(mean_square + norm_eps)
    if scales is not None:
        scaled = scaled * scales[None, :, None]
    return scaled.reshape(rows, -1).astype(jnp.bfloat16)


def attention_kernel(q_ref, kv_ref, o_ref):
    @pl.when(pl.program_id(0) == 0)
    def _():
        o_ref[...] = jnp.zeros_like(o_ref)

    q_step = min(QUERY_STEP, q_ref.shape[0])
    k_step = min(KEY_STEP, kv_ref.shape[0])
    q_count = q_ref.shape[0] // q_step
    k_count = kv_ref.shape[0] // k_step

    def body(turn, carry):
        rows = pl.ds(pl.multiple_of((turn // k_count) * q_step, q_step), q_step)
        keys = pl.ds(pl.multiple_of((turn % k_count) * k_step, k_step), k_step)
        block = kv_ref[keys, :]
        scores = lax.dot_general(
            q_ref[rows, :], block, (((1,), (1,)), ((), ())), preferred_element_type=jnp.float32
        )
        weights = jnp.exp(scores).astype(jnp.bfloat16)
        lane = lax.broadcasted_iota(jnp.int32, block.shape, 1)
        widened = jnp.where(lane < SUBSPACE_WIDTH, jnp.ones_like(block), block)
        o_ref[rows, :] += jnp.dot(weights, widened, preferred_element_type=jnp.float32)
        return carry

    lax.fori_loop(0, q_count * k_count, body, 0)


def attend(padded_queries, key_values):
    rows, width = padded_queries.shape
    keys = key_values.shape[0]
    block = min(KEY_BLOCK, keys)
    flops = 4 * rows * keys * width
    return pl.pallas_call(
        attention_kernel,
        grid=(keys // block,),
        in_specs=[
            pl.BlockSpec((rows, width), lambda j: (0, 0)),
            pl.BlockSpec((block, width), lambda j: (j, 0)),
        ],
        out_specs=pl.BlockSpec((rows, width), lambda j: (0, 0)),
        out_shape=jax.ShapeDtypeStruct((rows, width), jnp.float32),
        compiler_params=pltpu.CompilerParams(dimension_semantics=("arbitrary",)),
        cost_estimate=pl.CostEstimate(
            flops=flops, transcendentals=rows * keys, bytes_accessed=2 * keys * width + 6 * rows * width
        ),
    )(padded_queries, key_values)


def shards(
    vertex_embeddings,
    adjacent_group_bank_ids,
    coupling_strength_panels,
    asking_projector,
    lookup_projector,
    content_projector,
    final_projector,
    passing_inner_coefficients,
    passing_outer_coefficients,
    softness_per_subspace,
    mixing_layer_gain,
):
    block_len = vertex_embeddings.shape[0]
    group_size = lax.axis_size("head")
    pair_size = lax.axis_size(PAIR)
    members = group_size * pair_size
    slot_ids = adjacent_group_bank_ids.reshape(-1)
    halo_rows = extended(vertex_embeddings, block_len)
    me = lax.axis_index("head")
    gathered = [halo_rows]
    for shift in range(1, group_size):
        pairs = [(i, (i + shift) % group_size) for i in range(group_size)]
        gathered.append(lax.ppermute(halo_rows, "head", pairs))
    stacked = jnp.stack(gathered)
    order = (me - jnp.arange(group_size)) % group_size
    nearby = jnp.zeros_like(stacked).at[order].set(stacked).reshape(-1, halo_rows.shape[1])
    slot_order = slot_ids.reshape(3, group_size).T.reshape(-1)
    asking_vector_multiplier = softness_per_subspace / math.sqrt(SUBSPACE_WIDTH)
    keys_all = head_norm(
        jnp.dot(vertex_embeddings, lookup_projector, preferred_element_type=jnp.float32), None
    )
    values_all = jnp.dot(
        vertex_embeddings, content_projector, preferred_element_type=jnp.float32
    ).astype(jnp.bfloat16)

    head_of = [(j % group_size) * pair_size + j // group_size for j in range(members)]
    member_of = [head_of.index(h) for h in range(NUM_SUBSPACES)]

    def to_members(parts):
        packed = jnp.stack(
            [t.reshape(block_len, NUM_SUBSPACES, SUBSPACE_WIDTH) for t in parts], axis=2
        )[:, jnp.array(head_of)]
        return lax.all_to_all(
            packed.reshape(block_len, -1), GROUP, split_axis=1, concat_axis=0, tiled=True
        )

    me = lax.axis_index(PAIR) * group_size + lax.axis_index("head")
    kv_packed = jnp.stack(
        [t.reshape(block_len, NUM_SUBSPACES, SUBSPACE_WIDTH) for t in (keys_all, values_all)],
        axis=2,
    )[:, jnp.array(head_of)]
    pieces = [jnp.take(kv_packed, me, axis=1).reshape(block_len, -1)]
    for shift in range(1, members):
        chunk = jnp.take(kv_packed, lax.rem(me + shift, members), axis=1).reshape(block_len, -1)
        pairs = [(i, (i + shift) % members) for i in range(members)]
        pieces.append(lax.ppermute(chunk, GROUP, pairs))
    key_values = jnp.concatenate(pieces, axis=0)
    kv_in = lax.all_gather(key_values, (ROW, COLUMN), axis=0, tiled=True)
    queries = head_norm(
        jnp.dot(vertex_embeddings, asking_projector, preferred_element_type=jnp.float32),
        asking_vector_multiplier,
    )
    head_queries = to_members((queries,))
    query_rows = head_queries.shape[0]

    selected = jnp.take(coupling_strength_panels, jnp.maximum(slot_order, 0), axis=0)
    selected = jnp.where((slot_order >= 0)[:, None, None], selected, jnp.zeros_like(selected))
    wide_tiles = jnp.transpose(selected, (1, 0, 2)).reshape(block_len, -1)
    aggregate = jnp.dot(wide_tiles, nearby, preferred_element_type=jnp.float32).astype(jnp.bfloat16)
    hidden = jax.nn.gelu(
        jnp.dot(aggregate, passing_inner_coefficients, preferred_element_type=jnp.float32)
    ).astype(jnp.bfloat16)
    local_term = jnp.dot(hidden, passing_outer_coefficients, preferred_element_type=jnp.float32)

    local_term, head_queries = lax.optimization_barrier((local_term, head_queries))
    padded_queries = jnp.concatenate([head_queries, jnp.zeros_like(head_queries)], axis=1)
    totals = attend(padded_queries, kv_in)
    merged = (totals[:, SUBSPACE_WIDTH:] / totals[:, :1]).astype(jnp.bfloat16)
    back = lax.all_to_all(merged, GROUP, split_axis=0, concat_axis=1, tiled=True)
    node_heads = back.reshape(block_len, members, SUBSPACE_WIDTH)[:, jnp.array(member_of)]
    node_heads = node_heads.reshape(block_len, -1)
    attended = jnp.dot(node_heads, final_projector, preferred_element_type=jnp.float32)
    normed = (
        attended
        * lax.rsqrt(jnp.mean(attended * attended, axis=-1, keepdims=True) + norm_eps)
        * mixing_layer_gain
    )
    return (vertex_embeddings.astype(jnp.float32) + local_term + normed).astype(jnp.bfloat16)


def solution(mesh):
    n_dom, n_head = mesh.shape["dom"], mesh.shape["head"]
    fine = Mesh(mesh.devices.reshape(n_dom // 16, 8, 2, n_head), (ROW, COLUMN, PAIR, "head"))
    in_specs = (
        P((ROW, COLUMN, PAIR, "head"), None),
        P(DOM, "head", None),
        P(),
        P(),
        P(),
        P(),
        P(),
        P(),
        P(),
        P(),
        P(),
    )
    out_specs = P((ROW, COLUMN, PAIR, "head"), None)
    return jax.shard_map(shards, mesh=fine, in_specs=in_specs, out_specs=out_specs, check_vma=False)
```

```python
import math

import jax
from jax.experimental import pallas as pl
from jax.experimental.pallas import tpu as pltpu
import jax.numpy as jnp
from jax import lax
from jax.sharding import Mesh
from jax.sharding import PartitionSpec as P

NUM_SUBSPACES = 8
SUBSPACE_WIDTH = 64
KEY_BLOCK = 8192
KEY_STEP = 2048
QUERY_STEP = 1024

norm_eps = 1e-06

ROW = "x"
COLUMN = "z"
PAIR = "yhi"
DOM = (ROW, COLUMN, PAIR)
GROUP = (PAIR, "head")


def extended(shard, width):
    devices = lax.axis_size(ROW) * lax.axis_size(COLUMN) * lax.axis_size(PAIR)
    length = shard.shape[0]
    up = [(i, (i + 1) % devices) for i in range(devices - 1)]
    down = [(j, i) for i, j in up]
    last = lax.slice_in_dim(shard, length - width, length, axis=0)
    first = lax.slice_in_dim(shard, 0, width, axis=0)
    before = lax.ppermute(last, DOM, up)
    after = lax.ppermute(first, DOM, down)
    return jnp.concatenate([before, shard, after], axis=0)


def head_norm(projected, scales):
    rows = projected.shape[0]
    grouped = projected.reshape(rows, -1, SUBSPACE_WIDTH)
    mean_square = jnp.mean(grouped * grouped, axis=-1, keepdims=True)
    scaled = grouped * lax.rsqrt(mean_square + norm_eps)
    if scales is not None:
        scaled = scaled * scales[None, :, None]
    return scaled.reshape(rows, -1).astype(jnp.bfloat16)


def attention_kernel(q_ref, kv_ref, o_ref):
    @pl.when(pl.program_id(0) == 0)
    def _():
        o_ref[...] = jnp.zeros_like(o_ref)

    q_step = min(QUERY_STEP, q_ref.shape[0])
    k_step = min(KEY_STEP, kv_ref.shape[0])
    q_count = q_ref.shape[0] // q_step
    k_count = kv_ref.shape[0] // k_step

    def body(turn, carry):
        rows = pl.ds(pl.multiple_of((turn // k_count) * q_step, q_step), q_step)
        keys = pl.ds(pl.multiple_of((turn % k_count) * k_step, k_step), k_step)
        block = kv_ref[keys, :]
        scores = lax.dot_general(
            q_ref[rows, :], block, (((1,), (1,)), ((), ())), preferred_element_type=jnp.float32
        )
        weights = jnp.exp(scores).astype(jnp.bfloat16)
        lane = lax.broadcasted_iota(jnp.int32, block.shape, 1)
        widened = jnp.where(lane < SUBSPACE_WIDTH, jnp.ones_like(block), block)
        o_ref[rows, :] += jnp.dot(weights, widened, preferred_element_type=jnp.float32)
        return carry

    lax.fori_loop(0, q_count * k_count, body, 0)


def attend(padded_queries, key_values):
    rows, width = padded_queries.shape
    keys = key_values.shape[0]
    block = min(KEY_BLOCK, keys)
    flops = 4 * rows * keys * width
    return pl.pallas_call(
        attention_kernel,
        grid=(keys // block,),
        in_specs=[
            pl.BlockSpec((rows, width), lambda j: (0, 0)),
            pl.BlockSpec((block, width), lambda j: (j, 0)),
        ],
        out_specs=pl.BlockSpec((rows, width), lambda j: (0, 0)),
        out_shape=jax.ShapeDtypeStruct((rows, width), jnp.float32),
        compiler_params=pltpu.CompilerParams(dimension_semantics=("arbitrary",)),
        cost_estimate=pl.CostEstimate(
            flops=flops, transcendentals=rows * keys, bytes_accessed=2 * keys * width + 6 * rows * width
        ),
    )(padded_queries, key_values)


def shards(
    vertex_embeddings,
    adjacent_group_bank_ids,
    coupling_strength_panels,
    asking_projector,
    lookup_projector,
    content_projector,
    final_projector,
    passing_inner_coefficients,
    passing_outer_coefficients,
    softness_per_subspace,
    mixing_layer_gain,
):
    block_len = vertex_embeddings.shape[0]
    group_size = lax.axis_size("head")
    pair_size = lax.axis_size(PAIR)
    members = group_size * pair_size
    slot_ids = adjacent_group_bank_ids.reshape(-1)
    halo_rows = extended(vertex_embeddings, block_len)
    me = lax.axis_index("head")
    gathered = [halo_rows]
    for shift in range(1, group_size):
        pairs = [(i, (i + shift) % group_size) for i in range(group_size)]
        gathered.append(lax.ppermute(halo_rows, "head", pairs))
    stacked = jnp.stack(gathered)
    order = (me - jnp.arange(group_size)) % group_size
    nearby = jnp.zeros_like(stacked).at[order].set(stacked).reshape(-1, halo_rows.shape[1])
    slot_order = slot_ids.reshape(3, group_size).T.reshape(-1)
    asking_vector_multiplier = softness_per_subspace / math.sqrt(SUBSPACE_WIDTH)
    keys_all = head_norm(
        jnp.dot(vertex_embeddings, lookup_projector, preferred_element_type=jnp.float32), None
    )
    values_all = jnp.dot(
        vertex_embeddings, content_projector, preferred_element_type=jnp.float32
    ).astype(jnp.bfloat16)

    head_of = [(j % group_size) * pair_size + j // group_size for j in range(members)]
    member_of = [head_of.index(h) for h in range(NUM_SUBSPACES)]

    def to_members(parts):
        packed = jnp.stack(
            [t.reshape(block_len, NUM_SUBSPACES, SUBSPACE_WIDTH) for t in parts], axis=2
        )[:, jnp.array(head_of)]
        return lax.all_to_all(
            packed.reshape(block_len, -1), GROUP, split_axis=1, concat_axis=0, tiled=True
        )

    key_values = to_members((keys_all, values_all))
    kv_in = lax.all_gather(key_values, (COLUMN, ROW), axis=0, tiled=True)
    queries = head_norm(
        jnp.dot(vertex_embeddings, asking_projector, preferred_element_type=jnp.float32),
        asking_vector_multiplier,
    )
    head_queries = to_members((queries,))
    query_rows = head_queries.shape[0]

    selected = jnp.take(coupling_strength_panels, jnp.maximum(slot_order, 0), axis=0)
    selected = jnp.where((slot_order >= 0)[:, None, None], selected, jnp.zeros_like(selected))
    wide_tiles = jnp.transpose(selected, (1, 0, 2)).reshape(block_len, -1)
    aggregate = jnp.dot(wide_tiles, nearby, preferred_element_type=jnp.float32).astype(jnp.bfloat16)
    hidden = jax.nn.gelu(
        jnp.dot(aggregate, passing_inner_coefficients, preferred_element_type=jnp.float32)
    ).astype(jnp.bfloat16)
    local_term = jnp.dot(hidden, passing_outer_coefficients, preferred_element_type=jnp.float32)

    local_term, head_queries = lax.optimization_barrier((local_term, head_queries))
    padded_queries = jnp.concatenate([head_queries, jnp.zeros_like(head_queries)], axis=1)
    totals = attend(padded_queries, kv_in)
    merged = (totals[:, SUBSPACE_WIDTH:] / totals[:, :1]).astype(jnp.bfloat16)
    back = lax.all_to_all(merged, GROUP, split_axis=0, concat_axis=1, tiled=True)
    node_heads = back.reshape(block_len, members, SUBSPACE_WIDTH)[:, jnp.array(member_of)]
    node_heads = node_heads.reshape(block_len, -1)
    attended = jnp.dot(node_heads, final_projector, preferred_element_type=jnp.float32)
    normed = (
        attended
        * lax.rsqrt(jnp.mean(attended * attended, axis=-1, keepdims=True) + norm_eps)
        * mixing_layer_gain
    )
    return (vertex_embeddings.astype(jnp.float32) + local_term + normed).astype(jnp.bfloat16)


def solution(mesh):
    n_dom, n_head = mesh.shape["dom"], mesh.shape["head"]
    fine = Mesh(mesh.devices.reshape(n_dom // 16, 8, 2, n_head), (ROW, COLUMN, PAIR, "head"))
    in_specs = (
        P((ROW, COLUMN, PAIR, "head"), None),
        P(DOM, "head", None),
        P(),
        P(),
        P(),
        P(),
        P(),
        P(),
        P(),
        P(),
        P(),
    )
    out_specs = P((ROW, COLUMN, PAIR, "head"), None)
    return jax.shard_map(shards, mesh=fine, in_specs=in_specs, out_specs=out_specs, check_vma=False)
```

```python
import math

import jax
from jax.experimental import pallas as pl
from jax.experimental.pallas import tpu as pltpu
import jax.numpy as jnp
from jax import lax
from jax.sharding import Mesh
from jax.sharding import PartitionSpec as P

NUM_SUBSPACES = 8
SUBSPACE_WIDTH = 64
KEY_STEP = 2048

norm_eps = 1e-06

ROW = "x"
COLUMN = "z"
PAIR = "yhi"
DOM = (ROW, COLUMN, PAIR)
GROUP = (PAIR, "head")


def extended(shard, width):
    devices = lax.axis_size(ROW) * lax.axis_size(COLUMN) * lax.axis_size(PAIR)
    length = shard.shape[0]
    up = [(i, (i + 1) % devices) for i in range(devices - 1)]
    down = [(j, i) for i, j in up]
    last = lax.slice_in_dim(shard, length - width, length, axis=0)
    first = lax.slice_in_dim(shard, 0, width, axis=0)
    before = lax.ppermute(last, DOM, up)
    after = lax.ppermute(first, DOM, down)
    return jnp.concatenate([before, shard, after], axis=0)


def head_norm(projected, scales):
    rows = projected.shape[0]
    grouped = projected.reshape(rows, -1, SUBSPACE_WIDTH)
    mean_square = jnp.mean(grouped * grouped, axis=-1, keepdims=True)
    scaled = grouped * lax.rsqrt(mean_square + norm_eps)
    if scales is not None:
        scaled = scaled * scales[None, :, None]
    return scaled.reshape(rows, -1).astype(jnp.bfloat16)


def accumulate(q_ref, block, o_ref):
    step = min(KEY_STEP, block.shape[0])

    def body(turn, carry):
        keys = pl.ds(pl.multiple_of(turn * step, step), step)
        part = block[keys, :]
        scores = lax.dot_general(
            q_ref[...], part, (((1,), (1,)), ((), ())), preferred_element_type=jnp.float32
        )
        weights = jnp.exp(scores).astype(jnp.bfloat16)
        lane = lax.broadcasted_iota(jnp.int32, part.shape, 1)
        widened = jnp.where(lane < SUBSPACE_WIDTH, jnp.ones_like(part), part)
        o_ref[...] += jnp.dot(weights, widened, preferred_element_type=jnp.float32)
        return carry

    lax.fori_loop(0, block.shape[0] // step, body, 0)


def ring_kernel(q_ref, kv_ref, o_ref, slots, send_sem, recv_sem):
    positions = lax.axis_size(ROW)
    me = lax.axis_index(ROW)
    column = lax.axis_index(COLUMN)
    pair = lax.axis_index(PAIR)
    member = lax.axis_index("head")
    offsets = [1, positions - 1] + list(range(2, positions - 1))

    def copy_to(offset):
        target = lax.rem(me + offset, positions)
        return pltpu.make_async_remote_copy(
            src_ref=kv_ref,
            dst_ref=slots.at[me],
            send_sem=send_sem.at[offset],
            recv_sem=recv_sem.at[me],
            device_id=(target, column, pair, member),
            device_id_type=pl.DeviceIdType.MESH,
        )

    def arrival(offset):
        source = lax.rem(me - offset + positions, positions)
        return source, pltpu.make_async_remote_copy(
            src_ref=kv_ref,
            dst_ref=slots.at[source],
            send_sem=send_sem.at[offset],
            recv_sem=recv_sem.at[source],
            device_id=(source, column, pair, member),
            device_id_type=pl.DeviceIdType.MESH,
        )

    for offset in offsets:
        copy_to(offset).start()
    o_ref[...] = jnp.zeros_like(o_ref)
    accumulate(q_ref, kv_ref, o_ref)
    for offset in offsets:
        source, landing = arrival(offset)
        landing.wait_recv()
        accumulate(q_ref, slots.at[source], o_ref)
    for offset in offsets:
        copy_to(offset).wait_send()


def ring_attend(padded_queries, key_values):
    rows, width = padded_queries.shape
    positions = lax.axis_size(ROW)
    keys = positions * key_values.shape[0]
    return pl.pallas_call(
        ring_kernel,
        in_specs=[pl.BlockSpec(memory_space=pltpu.VMEM)] * 2,
        out_specs=pl.BlockSpec(memory_space=pltpu.VMEM),
        out_shape=jax.ShapeDtypeStruct((rows, width), jnp.float32),
        scratch_shapes=[
            pltpu.VMEM((positions,) + key_values.shape, key_values.dtype),
            pltpu.SemaphoreType.DMA((positions,)),
            pltpu.SemaphoreType.DMA((positions,)),
        ],
        compiler_params=pltpu.CompilerParams(has_side_effects=True),
        cost_estimate=pl.CostEstimate(
            flops=4 * rows * keys * width,
            transcendentals=rows * keys,
            bytes_accessed=2 * keys * width + 6 * rows * width,
        ),
    )(padded_queries, key_values)


def shards(
    vertex_embeddings,
    adjacent_group_bank_ids,
    coupling_strength_panels,
    asking_projector,
    lookup_projector,
    content_projector,
    final_projector,
    passing_inner_coefficients,
    passing_outer_coefficients,
    softness_per_subspace,
    mixing_layer_gain,
):
    block_len = vertex_embeddings.shape[0]
    group_size = lax.axis_size("head")
    pair_size = lax.axis_size(PAIR)
    members = group_size * pair_size
    slot_ids = adjacent_group_bank_ids.reshape(-1)
    halo_rows = extended(vertex_embeddings, block_len)
    me = lax.axis_index("head")
    gathered = [halo_rows]
    for shift in range(1, group_size):
        pairs = [(i, (i + shift) % group_size) for i in range(group_size)]
        gathered.append(lax.ppermute(halo_rows, "head", pairs))
    stacked = jnp.stack(gathered)
    order = (me - jnp.arange(group_size)) % group_size
    nearby = jnp.zeros_like(stacked).at[order].set(stacked).reshape(-1, halo_rows.shape[1])
    slot_order = slot_ids.reshape(3, group_size).T.reshape(-1)
    asking_vector_multiplier = softness_per_subspace / math.sqrt(SUBSPACE_WIDTH)
    keys_all = head_norm(
        jnp.dot(vertex_embeddings, lookup_projector, preferred_element_type=jnp.float32), None
    )
    values_all = jnp.dot(
        vertex_embeddings, content_projector, preferred_element_type=jnp.float32
    ).astype(jnp.bfloat16)

    head_of = [(j % group_size) * pair_size + j // group_size for j in range(members)]
    member_of = [head_of.index(h) for h in range(NUM_SUBSPACES)]

    def to_members(parts):
        packed = jnp.stack(
            [t.reshape(block_len, NUM_SUBSPACES, SUBSPACE_WIDTH) for t in parts], axis=2
        )[:, jnp.array(head_of)]
        return lax.all_to_all(
            packed.reshape(block_len, -1), GROUP, split_axis=1, concat_axis=0, tiled=True
        )

    key_values = to_members((keys_all, values_all))
    kv_in = lax.all_gather(key_values, COLUMN, axis=0, tiled=True)
    queries = head_norm(
        jnp.dot(vertex_embeddings, asking_projector, preferred_element_type=jnp.float32),
        asking_vector_multiplier,
    )
    head_queries = to_members((queries,))
    query_rows = head_queries.shape[0]

    selected = jnp.take(coupling_strength_panels, jnp.maximum(slot_order, 0), axis=0)
    selected = jnp.where((slot_order >= 0)[:, None, None], selected, jnp.zeros_like(selected))
    wide_tiles = jnp.transpose(selected, (1, 0, 2)).reshape(block_len, -1)
    aggregate = jnp.dot(wide_tiles, nearby, preferred_element_type=jnp.float32).astype(jnp.bfloat16)
    hidden = jax.nn.gelu(
        jnp.dot(aggregate, passing_inner_coefficients, preferred_element_type=jnp.float32)
    ).astype(jnp.bfloat16)
    local_term = jnp.dot(hidden, passing_outer_coefficients, preferred_element_type=jnp.float32)

    local_term, head_queries = lax.optimization_barrier((local_term, head_queries))
    padded_queries = jnp.concatenate([head_queries, jnp.zeros_like(head_queries)], axis=1)
    totals = ring_attend(padded_queries, kv_in)
    merged = (totals[:, SUBSPACE_WIDTH:] / totals[:, :1]).astype(jnp.bfloat16)
    back = lax.all_to_all(merged, GROUP, split_axis=0, concat_axis=1, tiled=True)
    node_heads = back.reshape(block_len, members, SUBSPACE_WIDTH)[:, jnp.array(member_of)]
    node_heads = node_heads.reshape(block_len, -1)
    attended = jnp.dot(node_heads, final_projector, preferred_element_type=jnp.float32)
    normed = (
        attended
        * lax.rsqrt(jnp.mean(attended * attended, axis=-1, keepdims=True) + norm_eps)
        * mixing_layer_gain
    )
    return (vertex_embeddings.astype(jnp.float32) + local_term + normed).astype(jnp.bfloat16)


def solution(mesh):
    n_dom, n_head = mesh.shape["dom"], mesh.shape["head"]
    fine = Mesh(mesh.devices.reshape(n_dom // 16, 8, 2, n_head), (ROW, COLUMN, PAIR, "head"))
    in_specs = (
        P((ROW, COLUMN, PAIR, "head"), None),
        P(DOM, "head", None),
        P(),
        P(),
        P(),
        P(),
        P(),
        P(),
        P(),
        P(),
        P(),
    )
    out_specs = P((ROW, COLUMN, PAIR, "head"), None)
    return jax.shard_map(shards, mesh=fine, in_specs=in_specs, out_specs=out_specs, check_vma=False)
```

```python
import math

import jax
from jax.experimental import pallas as pl
from jax.experimental.pallas import tpu as pltpu
import jax.numpy as jnp
from jax import lax
from jax.sharding import Mesh
from jax.sharding import PartitionSpec as P

NUM_SUBSPACES = 8
SUBSPACE_WIDTH = 64
KEY_BLOCK = 8192
KEY_STEP = 2048
QUERY_STEP = 1024

norm_eps = 1e-06

ROW = "x"
COLUMN = "z"
PAIR = "yhi"
DOM = (ROW, COLUMN, PAIR)
GROUP = (PAIR, "head")


def extended(shard, width):
    devices = lax.axis_size(ROW) * lax.axis_size(COLUMN) * lax.axis_size(PAIR)
    length = shard.shape[0]
    up = [(i, (i + 1) % devices) for i in range(devices - 1)]
    down = [(j, i) for i, j in up]
    last = lax.slice_in_dim(shard, length - width, length, axis=0)
    first = lax.slice_in_dim(shard, 0, width, axis=0)
    before = lax.ppermute(last, DOM, up)
    after = lax.ppermute(first, DOM, down)
    return jnp.concatenate([before, shard, after], axis=0)


def head_norm(projected, scales):
    rows = projected.shape[0]
    grouped = projected.reshape(rows, -1, SUBSPACE_WIDTH)
    mean_square = jnp.mean(grouped * grouped, axis=-1, keepdims=True)
    scaled = grouped * lax.rsqrt(mean_square + norm_eps)
    if scales is not None:
        scaled = scaled * scales[None, :, None]
    return scaled.reshape(rows, -1).astype(jnp.bfloat16)


def attention_kernel(q_ref, kv_ref, o_ref, acc_ref):
    @pl.when(pl.program_id(0) == 0)
    def _():
        acc_ref[...] = jnp.zeros_like(acc_ref)

    q_step = min(QUERY_STEP, q_ref.shape[0])
    k_step = min(KEY_STEP, kv_ref.shape[0])
    q_count = q_ref.shape[0] // q_step
    k_count = kv_ref.shape[0] // k_step

    def body(turn, carry):
        rows = pl.ds(pl.multiple_of((turn // k_count) * q_step, q_step), q_step)
        keys = pl.ds(pl.multiple_of((turn % k_count) * k_step, k_step), k_step)
        block = kv_ref[keys, :]
        scores = lax.dot_general(
            q_ref[rows, :], block, (((1,), (1,)), ((), ())), preferred_element_type=jnp.float32
        )
        weights = jnp.exp(scores).astype(jnp.bfloat16)
        lane = lax.broadcasted_iota(jnp.int32, block.shape, 1)
        widened = jnp.where(lane < SUBSPACE_WIDTH, jnp.ones_like(block), block)
        acc_ref[rows, :] += jnp.dot(weights, widened, preferred_element_type=jnp.float32)
        return carry

    lax.fori_loop(0, q_count * k_count, body, 0)

    @pl.when(pl.program_id(0) == pl.num_programs(0) - 1)
    def _():
        totals = acc_ref[...]
        o_ref[...] = (totals[:, SUBSPACE_WIDTH:] / totals[:, :1]).astype(o_ref.dtype)


def attend(padded_queries, key_values):
    rows, width = padded_queries.shape
    keys = key_values.shape[0]
    block = min(KEY_BLOCK, keys)
    flops = 4 * rows * keys * width
    return pl.pallas_call(
        attention_kernel,
        grid=(keys // block,),
        in_specs=[
            pl.BlockSpec((rows, width), lambda j: (0, 0)),
            pl.BlockSpec((block, width), lambda j: (j, 0)),
        ],
        out_specs=pl.BlockSpec((rows, SUBSPACE_WIDTH), lambda j: (0, 0)),
        out_shape=jax.ShapeDtypeStruct((rows, SUBSPACE_WIDTH), jnp.bfloat16),
        scratch_shapes=[pltpu.VMEM((rows, width), jnp.float32)],
        compiler_params=pltpu.CompilerParams(dimension_semantics=("arbitrary",)),
        cost_estimate=pl.CostEstimate(
            flops=flops, transcendentals=rows * keys, bytes_accessed=2 * keys * width + 6 * rows * width
        ),
    )(padded_queries, key_values)


def shards(
    vertex_embeddings,
    adjacent_group_bank_ids,
    coupling_strength_panels,
    asking_projector,
    lookup_projector,
    content_projector,
    final_projector,
    passing_inner_coefficients,
    passing_outer_coefficients,
    softness_per_subspace,
    mixing_layer_gain,
):
    block_len = vertex_embeddings.shape[0]
    group_size = lax.axis_size("head")
    pair_size = lax.axis_size(PAIR)
    members = group_size * pair_size
    slot_ids = adjacent_group_bank_ids.reshape(-1)
    halo_rows = extended(vertex_embeddings, block_len)
    me = lax.axis_index("head")
    gathered = [halo_rows]
    for shift in range(1, group_size):
        pairs = [(i, (i + shift) % group_size) for i in range(group_size)]
        gathered.append(lax.ppermute(halo_rows, "head", pairs))
    stacked = jnp.stack(gathered)
    order = (me - jnp.arange(group_size)) % group_size
    nearby = jnp.zeros_like(stacked).at[order].set(stacked).reshape(-1, halo_rows.shape[1])
    slot_order = slot_ids.reshape(3, group_size).T.reshape(-1)
    asking_vector_multiplier = softness_per_subspace / math.sqrt(SUBSPACE_WIDTH)
    keys_all = head_norm(
        jnp.dot(vertex_embeddings, lookup_projector, preferred_element_type=jnp.float32), None
    )
    values_all = jnp.dot(
        vertex_embeddings, content_projector, preferred_element_type=jnp.float32
    ).astype(jnp.bfloat16)

    head_of = [(j % group_size) * pair_size + j // group_size for j in range(members)]
    member_of = [head_of.index(h) for h in range(NUM_SUBSPACES)]

    def to_members(parts):
        packed = jnp.stack(
            [t.reshape(block_len, NUM_SUBSPACES, SUBSPACE_WIDTH) for t in parts], axis=2
        )[:, jnp.array(head_of)]
        return lax.all_to_all(
            packed.reshape(block_len, -1), GROUP, split_axis=1, concat_axis=0, tiled=True
        )

    key_values = to_members((keys_all, values_all))
    kv_in = lax.all_gather(key_values, (COLUMN, ROW), axis=0, tiled=True)
    queries = head_norm(
        jnp.dot(vertex_embeddings, asking_projector, preferred_element_type=jnp.float32),
        asking_vector_multiplier,
    )
    head_queries = to_members((queries,))
    query_rows = head_queries.shape[0]

    selected = jnp.take(coupling_strength_panels, jnp.maximum(slot_order, 0), axis=0)
    selected = jnp.where((slot_order >= 0)[:, None, None], selected, jnp.zeros_like(selected))
    wide_tiles = jnp.transpose(selected, (1, 0, 2)).reshape(block_len, -1)
    aggregate = jnp.dot(wide_tiles, nearby, preferred_element_type=jnp.float32).astype(jnp.bfloat16)
    hidden = jax.nn.gelu(
        jnp.dot(aggregate, passing_inner_coefficients, preferred_element_type=jnp.float32)
    ).astype(jnp.bfloat16)
    local_term = jnp.dot(hidden, passing_outer_coefficients, preferred_element_type=jnp.float32)

    local_term, head_queries = lax.optimization_barrier((local_term, head_queries))
    padded_queries = jnp.concatenate([head_queries, jnp.zeros_like(head_queries)], axis=1)
    merged = attend(padded_queries, kv_in)
    back = lax.all_to_all(merged, GROUP, split_axis=0, concat_axis=1, tiled=True)
    node_heads = back.reshape(block_len, members, SUBSPACE_WIDTH)[:, jnp.array(member_of)]
    node_heads = node_heads.reshape(block_len, -1)
    attended = jnp.dot(node_heads, final_projector, preferred_element_type=jnp.float32)
    normed = (
        attended
        * lax.rsqrt(jnp.mean(attended * attended, axis=-1, keepdims=True) + norm_eps)
        * mixing_layer_gain
    )
    return (vertex_embeddings.astype(jnp.float32) + local_term + normed).astype(jnp.bfloat16)


def solution(mesh):
    n_dom, n_head = mesh.shape["dom"], mesh.shape["head"]
    fine = Mesh(mesh.devices.reshape(n_dom // 16, 8, 2, n_head), (ROW, COLUMN, PAIR, "head"))
    in_specs = (
        P((ROW, COLUMN, PAIR, "head"), None),
        P(DOM, "head", None),
        P(),
        P(),
        P(),
        P(),
        P(),
        P(),
        P(),
        P(),
        P(),
    )
    out_specs = P((ROW, COLUMN, PAIR, "head"), None)
    return jax.shard_map(shards, mesh=fine, in_specs=in_specs, out_specs=out_specs, check_vma=False)
```

```python
import math

import jax
from jax.experimental import pallas as pl
from jax.experimental.pallas import tpu as pltpu
import jax.numpy as jnp
from jax import lax
from jax.sharding import Mesh
from jax.sharding import PartitionSpec as P

NUM_SUBSPACES = 8
SUBSPACE_WIDTH = 64
KEY_BLOCK = 8192
KEY_STEP = 4096
QUERY_STEP = 1024

norm_eps = 1e-06

ROW = "x"
COLUMN = "z"
PAIR = "yhi"
DOM = (ROW, COLUMN, PAIR)
GROUP = (PAIR, "head")


def extended(shard, width):
    devices = lax.axis_size(ROW) * lax.axis_size(COLUMN) * lax.axis_size(PAIR)
    length = shard.shape[0]
    up = [(i, (i + 1) % devices) for i in range(devices - 1)]
    down = [(j, i) for i, j in up]
    last = lax.slice_in_dim(shard, length - width, length, axis=0)
    first = lax.slice_in_dim(shard, 0, width, axis=0)
    before = lax.ppermute(last, DOM, up)
    after = lax.ppermute(first, DOM, down)
    return jnp.concatenate([before, shard, after], axis=0)


def head_norm(projected, scales):
    rows = projected.shape[0]
    grouped = projected.reshape(rows, -1, SUBSPACE_WIDTH)
    mean_square = jnp.mean(grouped * grouped, axis=-1, keepdims=True)
    scaled = grouped * lax.rsqrt(mean_square + norm_eps)
    if scales is not None:
        scaled = scaled * scales[None, :, None]
    return scaled.reshape(rows, -1).astype(jnp.bfloat16)


def attention_kernel(q_ref, kv_ref, o_ref, acc_ref):
    @pl.when(pl.program_id(0) == 0)
    def _():
        acc_ref[...] = jnp.zeros_like(acc_ref)

    q_step = min(QUERY_STEP, q_ref.shape[0])
    k_step = min(KEY_STEP, kv_ref.shape[0])
    q_count = q_ref.shape[0] // q_step
    k_count = kv_ref.shape[0] // k_step

    def body(turn, carry):
        rows = pl.ds(pl.multiple_of((turn // k_count) * q_step, q_step), q_step)
        keys = pl.ds(pl.multiple_of((turn % k_count) * k_step, k_step), k_step)
        block = kv_ref[keys, :]
        scores = lax.dot_general(
            q_ref[rows, :], block, (((1,), (1,)), ((), ())), preferred_element_type=jnp.float32
        )
        weights = jnp.exp(scores).astype(jnp.bfloat16)
        lane = lax.broadcasted_iota(jnp.int32, block.shape, 1)
        widened = jnp.where(lane < SUBSPACE_WIDTH, jnp.ones_like(block), block)
        acc_ref[rows, :] += jnp.dot(weights, widened, preferred_element_type=jnp.float32)
        return carry

    lax.fori_loop(0, q_count * k_count, body, 0)

    @pl.when(pl.program_id(0) == pl.num_programs(0) - 1)
    def _():
        totals = acc_ref[...]
        o_ref[...] = (totals[:, SUBSPACE_WIDTH:] / totals[:, :1]).astype(o_ref.dtype)


def attend(padded_queries, key_values):
    rows, width = padded_queries.shape
    keys = key_values.shape[0]
    block = min(KEY_BLOCK, keys)
    flops = 4 * rows * keys * width
    return pl.pallas_call(
        attention_kernel,
        grid=(keys // block,),
        in_specs=[
            pl.BlockSpec((rows, width), lambda j: (0, 0)),
            pl.BlockSpec((block, width), lambda j: (j, 0)),
        ],
        out_specs=pl.BlockSpec((rows, SUBSPACE_WIDTH), lambda j: (0, 0)),
        out_shape=jax.ShapeDtypeStruct((rows, SUBSPACE_WIDTH), jnp.bfloat16),
        scratch_shapes=[pltpu.VMEM((rows, width), jnp.float32)],
        compiler_params=pltpu.CompilerParams(dimension_semantics=("arbitrary",)),
        cost_estimate=pl.CostEstimate(
            flops=flops, transcendentals=rows * keys, bytes_accessed=2 * keys * width + 6 * rows * width
        ),
    )(padded_queries, key_values)


def shards(
    vertex_embeddings,
    adjacent_group_bank_ids,
    coupling_strength_panels,
    asking_projector,
    lookup_projector,
    content_projector,
    final_projector,
    passing_inner_coefficients,
    passing_outer_coefficients,
    softness_per_subspace,
    mixing_layer_gain,
):
    block_len = vertex_embeddings.shape[0]
    group_size = lax.axis_size("head")
    pair_size = lax.axis_size(PAIR)
    members = group_size * pair_size
    slot_ids = adjacent_group_bank_ids.reshape(-1)
    halo_rows = extended(vertex_embeddings, block_len)
    me = lax.axis_index("head")
    gathered = [halo_rows]
    for shift in range(1, group_size):
        pairs = [(i, (i + shift) % group_size) for i in range(group_size)]
        gathered.append(lax.ppermute(halo_rows, "head", pairs))
    stacked = jnp.stack(gathered)
    order = (me - jnp.arange(group_size)) % group_size
    nearby = jnp.zeros_like(stacked).at[order].set(stacked).reshape(-1, halo_rows.shape[1])
    slot_order = slot_ids.reshape(3, group_size).T.reshape(-1)
    asking_vector_multiplier = softness_per_subspace / math.sqrt(SUBSPACE_WIDTH)
    keys_all = head_norm(
        jnp.dot(vertex_embeddings, lookup_projector, preferred_element_type=jnp.float32), None
    )
    values_all = jnp.dot(
        vertex_embeddings, content_projector, preferred_element_type=jnp.float32
    ).astype(jnp.bfloat16)

    head_of = [(j % group_size) * pair_size + j // group_size for j in range(members)]
    member_of = [head_of.index(h) for h in range(NUM_SUBSPACES)]

    def to_members(parts):
        packed = jnp.stack(
            [t.reshape(block_len, NUM_SUBSPACES, SUBSPACE_WIDTH) for t in parts], axis=2
        )[:, jnp.array(head_of)]
        return lax.all_to_all(
            packed.reshape(block_len, -1), GROUP, split_axis=1, concat_axis=0, tiled=True
        )

    key_values = to_members((keys_all, values_all))
    kv_in = lax.all_gather(key_values, (COLUMN, ROW), axis=0, tiled=True)
    queries = head_norm(
        jnp.dot(vertex_embeddings, asking_projector, preferred_element_type=jnp.float32),
        asking_vector_multiplier,
    )
    head_queries = to_members((queries,))
    query_rows = head_queries.shape[0]

    selected = jnp.take(coupling_strength_panels, jnp.maximum(slot_order, 0), axis=0)
    selected = jnp.where((slot_order >= 0)[:, None, None], selected, jnp.zeros_like(selected))
    wide_tiles = jnp.transpose(selected, (1, 0, 2)).reshape(block_len, -1)
    aggregate = jnp.dot(wide_tiles, nearby, preferred_element_type=jnp.float32).astype(jnp.bfloat16)
    hidden = jax.nn.gelu(
        jnp.dot(aggregate, passing_inner_coefficients, preferred_element_type=jnp.float32)
    ).astype(jnp.bfloat16)
    local_term = jnp.dot(hidden, passing_outer_coefficients, preferred_element_type=jnp.float32)

    local_term, head_queries = lax.optimization_barrier((local_term, head_queries))
    padded_queries = jnp.concatenate([head_queries, jnp.zeros_like(head_queries)], axis=1)
    merged = attend(padded_queries, kv_in)
    back = lax.all_to_all(merged, GROUP, split_axis=0, concat_axis=1, tiled=True)
    node_heads = back.reshape(block_len, members, SUBSPACE_WIDTH)[:, jnp.array(member_of)]
    node_heads = node_heads.reshape(block_len, -1)
    attended = jnp.dot(node_heads, final_projector, preferred_element_type=jnp.float32)
    normed = (
        attended
        * lax.rsqrt(jnp.mean(attended * attended, axis=-1, keepdims=True) + norm_eps)
        * mixing_layer_gain
    )
    return (vertex_embeddings.astype(jnp.float32) + local_term + normed).astype(jnp.bfloat16)


def solution(mesh):
    n_dom, n_head = mesh.shape["dom"], mesh.shape["head"]
    fine = Mesh(mesh.devices.reshape(n_dom // 16, 8, 2, n_head), (ROW, COLUMN, PAIR, "head"))
    in_specs = (
        P((ROW, COLUMN, PAIR, "head"), None),
        P(DOM, "head", None),
        P(),
        P(),
        P(),
        P(),
        P(),
        P(),
        P(),
        P(),
        P(),
    )
    out_specs = P((ROW, COLUMN, PAIR, "head"), None)
    return jax.shard_map(shards, mesh=fine, in_specs=in_specs, out_specs=out_specs, check_vma=False)
```

```python
import math

import jax
from jax.experimental import pallas as pl
from jax.experimental.pallas import tpu as pltpu
import jax.numpy as jnp
from jax import lax
from jax.sharding import Mesh
from jax.sharding import PartitionSpec as P

NUM_SUBSPACES = 8
SUBSPACE_WIDTH = 64
KEY_BLOCK = 8192
KEY_STEP = 4096
QUERY_STEP = 1024

norm_eps = 1e-06

ROW = "x"
COLUMN = "z"
PAIR = "yhi"
DOM = (ROW, COLUMN, PAIR)
GROUP = (PAIR, "head")


def extended(shard, width):
    devices = lax.axis_size(ROW) * lax.axis_size(COLUMN) * lax.axis_size(PAIR)
    length = shard.shape[0]
    up = [(i, (i + 1) % devices) for i in range(devices - 1)]
    down = [(j, i) for i, j in up]
    last = lax.slice_in_dim(shard, length - width, length, axis=0)
    first = lax.slice_in_dim(shard, 0, width, axis=0)
    before = lax.ppermute(last, DOM, up)
    after = lax.ppermute(first, DOM, down)
    return jnp.concatenate([before, shard, after], axis=0)


def head_norm(projected, scales):
    rows = projected.shape[0]
    grouped = projected.reshape(rows, -1, SUBSPACE_WIDTH)
    mean_square = jnp.mean(grouped * grouped, axis=-1, keepdims=True)
    scaled = grouped * lax.rsqrt(mean_square + norm_eps)
    if scales is not None:
        scaled = scaled * scales[None, :, None]
    return scaled.reshape(rows, -1).astype(jnp.bfloat16)


def attention_kernel(q_ref, kv_ref, o_ref, acc_ref):
    @pl.when(pl.program_id(0) == 0)
    def _():
        acc_ref[...] = jnp.zeros_like(acc_ref)

    q_step = min(QUERY_STEP, q_ref.shape[0])
    k_step = min(KEY_STEP, kv_ref.shape[0])
    q_count = q_ref.shape[0] // q_step
    k_count = kv_ref.shape[0] // k_step

    def body(turn, carry):
        rows = pl.ds(pl.multiple_of((turn // k_count) * q_step, q_step), q_step)
        keys = pl.ds(pl.multiple_of((turn % k_count) * k_step, k_step), k_step)
        block = kv_ref[keys, :]
        scores = lax.dot_general(
            q_ref[rows, :], block, (((1,), (1,)), ((), ())), preferred_element_type=jnp.float32
        )
        weights = jnp.exp(scores).astype(jnp.bfloat16)
        lane = lax.broadcasted_iota(jnp.int32, block.shape, 1)
        widened = jnp.where(lane < SUBSPACE_WIDTH, jnp.ones_like(block), block)
        acc_ref[rows, :] += jnp.dot(weights, widened, preferred_element_type=jnp.float32)
        return carry

    lax.fori_loop(0, q_count * k_count, body, 0)

    @pl.when(pl.program_id(0) == pl.num_programs(0) - 1)
    def _():
        totals = acc_ref[...]
        o_ref[...] = (totals[:, SUBSPACE_WIDTH:] / totals[:, :1]).astype(o_ref.dtype)


def attend(padded_queries, key_values):
    rows, width = padded_queries.shape
    keys = key_values.shape[0]
    block = min(KEY_BLOCK, keys)
    flops = 4 * rows * keys * width
    return pl.pallas_call(
        attention_kernel,
        grid=(keys // block,),
        in_specs=[
            pl.BlockSpec((rows, width), lambda j: (0, 0)),
            pl.BlockSpec((block, width), lambda j: (j, 0)),
        ],
        out_specs=pl.BlockSpec((rows, SUBSPACE_WIDTH), lambda j: (0, 0)),
        out_shape=jax.ShapeDtypeStruct((rows, SUBSPACE_WIDTH), jnp.bfloat16),
        scratch_shapes=[pltpu.VMEM((rows, width), jnp.float32)],
        compiler_params=pltpu.CompilerParams(dimension_semantics=("arbitrary",)),
        cost_estimate=pl.CostEstimate(
            flops=flops, transcendentals=rows * keys, bytes_accessed=2 * keys * width + 6 * rows * width
        ),
    )(padded_queries, key_values)


def return_kernel(m_ref, o_ref, landing, send_sem, recv_sem):
    group_size = lax.axis_size("head")
    members = lax.axis_size(PAIR) * group_size
    me = lax.axis_index(PAIR) * group_size + lax.axis_index("head")
    row = lax.axis_index(ROW)
    column = lax.axis_index(COLUMN)
    rows = o_ref.shape[1]

    def device(t):
        return (row, column, t // group_size, lax.rem(t, group_size))

    barrier = pltpu.get_barrier_semaphore()
    for shift in range(1, members):
        pl.semaphore_signal(
            barrier, inc=1, device_id=device(lax.rem(me + shift, members)),
            device_id_type=pl.DeviceIdType.MESH,
        )
    pl.semaphore_wait(barrier, members - 1)

    def copy_to(shift):
        target = lax.rem(me + shift, members)
        return pltpu.make_async_remote_copy(
            src_ref=m_ref.at[pl.ds(pl.multiple_of(target * rows, rows), rows)],
            dst_ref=landing.at[me],
            send_sem=send_sem.at[shift],
            recv_sem=recv_sem.at[me],
            device_id=device(target),
            device_id_type=pl.DeviceIdType.MESH,
        )

    def arrival(shift):
        source = lax.rem(me - shift + members, members)
        return source, pltpu.make_async_remote_copy(
            src_ref=m_ref.at[pl.ds(0, rows)],
            dst_ref=landing.at[source],
            send_sem=send_sem.at[shift],
            recv_sem=recv_sem.at[source],
            device_id=device(source),
            device_id_type=pl.DeviceIdType.MESH,
        )

    for shift in range(1, members):
        copy_to(shift).start()
    o_ref[me] = m_ref[pl.ds(pl.multiple_of(me * rows, rows), rows), :]
    for shift in range(1, members):
        source, landed = arrival(shift)
        landed.wait_recv()
        o_ref[source] = landing[source]
    for shift in range(1, members):
        copy_to(shift).wait_send()


def return_pieces(merged, members):
    rows = merged.shape[0] // members
    piece = (members, rows, merged.shape[1])
    return pl.pallas_call(
        return_kernel,
        in_specs=[pl.BlockSpec(memory_space=pltpu.VMEM)],
        out_specs=pl.BlockSpec(memory_space=pltpu.VMEM),
        out_shape=jax.ShapeDtypeStruct(piece, merged.dtype),
        scratch_shapes=[
            pltpu.VMEM(piece, merged.dtype),
            pltpu.SemaphoreType.DMA((members,)),
            pltpu.SemaphoreType.DMA((members,)),
        ],
        compiler_params=pltpu.CompilerParams(collective_id=0, has_side_effects=True),
    )(merged)


def shards(
    vertex_embeddings,
    adjacent_group_bank_ids,
    coupling_strength_panels,
    asking_projector,
    lookup_projector,
    content_projector,
    final_projector,
    passing_inner_coefficients,
    passing_outer_coefficients,
    softness_per_subspace,
    mixing_layer_gain,
):
    block_len = vertex_embeddings.shape[0]
    group_size = lax.axis_size("head")
    pair_size = lax.axis_size(PAIR)
    members = group_size * pair_size
    slot_ids = adjacent_group_bank_ids.reshape(-1)
    halo_rows = extended(vertex_embeddings, block_len)
    me = lax.axis_index("head")
    gathered = [halo_rows]
    for shift in range(1, group_size):
        pairs = [(i, (i + shift) % group_size) for i in range(group_size)]
        gathered.append(lax.ppermute(halo_rows, "head", pairs))
    stacked = jnp.stack(gathered)
    order = (me - jnp.arange(group_size)) % group_size
    nearby = jnp.zeros_like(stacked).at[order].set(stacked).reshape(-1, halo_rows.shape[1])
    slot_order = slot_ids.reshape(3, group_size).T.reshape(-1)
    asking_vector_multiplier = softness_per_subspace / math.sqrt(SUBSPACE_WIDTH)
    keys_all = head_norm(
        jnp.dot(vertex_embeddings, lookup_projector, preferred_element_type=jnp.float32), None
    )
    values_all = jnp.dot(
        vertex_embeddings, content_projector, preferred_element_type=jnp.float32
    ).astype(jnp.bfloat16)

    head_of = [(j % group_size) * pair_size + j // group_size for j in range(members)]
    member_of = [head_of.index(h) for h in range(NUM_SUBSPACES)]

    def to_members(parts):
        packed = jnp.stack(
            [t.reshape(block_len, NUM_SUBSPACES, SUBSPACE_WIDTH) for t in parts], axis=2
        )[:, jnp.array(head_of)]
        return lax.all_to_all(
            packed.reshape(block_len, -1), GROUP, split_axis=1, concat_axis=0, tiled=True
        )

    key_values = to_members((keys_all, values_all))
    kv_in = lax.all_gather(key_values, (COLUMN, ROW), axis=0, tiled=True)
    queries = head_norm(
        jnp.dot(vertex_embeddings, asking_projector, preferred_element_type=jnp.float32),
        asking_vector_multiplier,
    )
    head_queries = to_members((queries,))
    query_rows = head_queries.shape[0]

    selected = jnp.take(coupling_strength_panels, jnp.maximum(slot_order, 0), axis=0)
    selected = jnp.where((slot_order >= 0)[:, None, None], selected, jnp.zeros_like(selected))
    wide_tiles = jnp.transpose(selected, (1, 0, 2)).reshape(block_len, -1)
    aggregate = jnp.dot(wide_tiles, nearby, preferred_element_type=jnp.float32).astype(jnp.bfloat16)
    hidden = jax.nn.gelu(
        jnp.dot(aggregate, passing_inner_coefficients, preferred_element_type=jnp.float32)
    ).astype(jnp.bfloat16)
    local_term = jnp.dot(hidden, passing_outer_coefficients, preferred_element_type=jnp.float32)

    local_term, head_queries = lax.optimization_barrier((local_term, head_queries))
    padded_queries = jnp.concatenate([head_queries, jnp.zeros_like(head_queries)], axis=1)
    merged = attend(padded_queries, kv_in)
    back = return_pieces(merged, members)
    node_heads = jnp.transpose(back, (1, 0, 2))[:, jnp.array(member_of)]
    node_heads = node_heads.reshape(block_len, -1)
    attended = jnp.dot(node_heads, final_projector, preferred_element_type=jnp.float32)
    normed = (
        attended
        * lax.rsqrt(jnp.mean(attended * attended, axis=-1, keepdims=True) + norm_eps)
        * mixing_layer_gain
    )
    return (vertex_embeddings.astype(jnp.float32) + local_term + normed).astype(jnp.bfloat16)


def solution(mesh):
    n_dom, n_head = mesh.shape["dom"], mesh.shape["head"]
    fine = Mesh(mesh.devices.reshape(n_dom // 16, 8, 2, n_head), (ROW, COLUMN, PAIR, "head"))
    in_specs = (
        P((ROW, COLUMN, PAIR, "head"), None),
        P(DOM, "head", None),
        P(),
        P(),
        P(),
        P(),
        P(),
        P(),
        P(),
        P(),
        P(),
    )
    out_specs = P((ROW, COLUMN, PAIR, "head"), None)
    return jax.shard_map(shards, mesh=fine, in_specs=in_specs, out_specs=out_specs, check_vma=False)
```

```python
import math

import jax
from jax.experimental import pallas as pl
from jax.experimental.pallas import tpu as pltpu
import jax.numpy as jnp
from jax import lax
from jax.sharding import Mesh
from jax.sharding import PartitionSpec as P

NUM_SUBSPACES = 8
SUBSPACE_WIDTH = 64
KEY_BLOCK = 8192
KEY_STEP = 4096
QUERY_STEP = 1024

norm_eps = 1e-06

ROW = "x"
COLUMN = "z"
PAIR = "yhi"
DOM = (ROW, COLUMN, PAIR)
GROUP = (PAIR, "head")


def extended(shard, width):
    devices = lax.axis_size(ROW) * lax.axis_size(COLUMN) * lax.axis_size(PAIR)
    length = shard.shape[0]
    up = [(i, (i + 1) % devices) for i in range(devices - 1)]
    down = [(j, i) for i, j in up]
    last = lax.slice_in_dim(shard, length - width, length, axis=0)
    first = lax.slice_in_dim(shard, 0, width, axis=0)
    before = lax.ppermute(last, DOM, up)
    after = lax.ppermute(first, DOM, down)
    return jnp.concatenate([before, shard, after], axis=0)


def head_norm(projected, scales):
    rows = projected.shape[0]
    grouped = projected.reshape(rows, -1, SUBSPACE_WIDTH)
    mean_square = jnp.mean(grouped * grouped, axis=-1, keepdims=True)
    scaled = grouped * lax.rsqrt(mean_square + norm_eps)
    if scales is not None:
        scaled = scaled * scales[None, :, None]
    return scaled.reshape(rows, -1).astype(jnp.bfloat16)


def attention_kernel(q_ref, kv_ref, o_ref, acc_ref):
    @pl.when(pl.program_id(0) == 0)
    def _():
        acc_ref[...] = jnp.zeros_like(acc_ref)

    q_step = min(QUERY_STEP, q_ref.shape[0])
    k_step = min(KEY_STEP, kv_ref.shape[0])
    q_count = q_ref.shape[0] // q_step
    k_count = kv_ref.shape[0] // k_step

    def body(turn, carry):
        rows = pl.ds(pl.multiple_of((turn // k_count) * q_step, q_step), q_step)
        keys = pl.ds(pl.multiple_of((turn % k_count) * k_step, k_step), k_step)
        block = kv_ref[keys, :]
        scores = lax.dot_general(
            q_ref[rows, :], block, (((1,), (1,)), ((), ())), preferred_element_type=jnp.float32
        )
        weights = jnp.exp(scores).astype(jnp.bfloat16)
        lane = lax.broadcasted_iota(jnp.int32, block.shape, 1)
        widened = jnp.where(lane < SUBSPACE_WIDTH, jnp.ones_like(block), block)
        acc_ref[rows, :] += jnp.dot(weights, widened, preferred_element_type=jnp.float32)
        return carry

    lax.fori_loop(0, q_count * k_count, body, 0)

    @pl.when(pl.program_id(0) == pl.num_programs(0) - 1)
    def _():
        totals = acc_ref[...]
        o_ref[...] = (totals[:, SUBSPACE_WIDTH:] / totals[:, :1]).astype(o_ref.dtype)


def attend(padded_queries, key_values):
    rows, width = padded_queries.shape
    keys = key_values.shape[0]
    block = min(KEY_BLOCK, keys)
    flops = 4 * rows * keys * width
    return pl.pallas_call(
        attention_kernel,
        grid=(keys // block,),
        in_specs=[
            pl.BlockSpec((rows, width), lambda j: (0, 0)),
            pl.BlockSpec((block, width), lambda j: (j, 0)),
        ],
        out_specs=pl.BlockSpec((rows, SUBSPACE_WIDTH), lambda j: (0, 0)),
        out_shape=jax.ShapeDtypeStruct((rows, SUBSPACE_WIDTH), jnp.bfloat16),
        scratch_shapes=[pltpu.VMEM((rows, width), jnp.float32)],
        compiler_params=pltpu.CompilerParams(dimension_semantics=("arbitrary",)),
        cost_estimate=pl.CostEstimate(
            flops=flops, transcendentals=rows * keys, bytes_accessed=2 * keys * width + 6 * rows * width
        ),
    )(padded_queries, key_values)


def return_kernel(m_ref, o_ref, landing, send_sem, recv_sem):
    group_size = lax.axis_size("head")
    members = lax.axis_size(PAIR) * group_size
    me = lax.axis_index(PAIR) * group_size + lax.axis_index("head")
    row = lax.axis_index(ROW)
    column = lax.axis_index(COLUMN)
    rows = o_ref.shape[1]

    def device(t):
        return (row, column, t // group_size, lax.rem(t, group_size))

    barrier = pltpu.get_barrier_semaphore()
    for shift in range(1, members):
        pl.semaphore_signal(
            barrier, inc=1, device_id=device(lax.rem(me + shift, members)),
            device_id_type=pl.DeviceIdType.MESH,
        )
    pl.semaphore_wait(barrier, members - 1)

    def copy_to(shift):
        target = lax.rem(me + shift, members)
        return pltpu.make_async_remote_copy(
            src_ref=m_ref.at[pl.ds(pl.multiple_of(target * rows, rows), rows)],
            dst_ref=landing.at[me],
            send_sem=send_sem.at[shift],
            recv_sem=recv_sem.at[me],
            device_id=device(target),
            device_id_type=pl.DeviceIdType.MESH,
        )

    def arrival(shift):
        source = lax.rem(me - shift + members, members)
        return source, pltpu.make_async_remote_copy(
            src_ref=m_ref.at[pl.ds(0, rows)],
            dst_ref=landing.at[source],
            send_sem=send_sem.at[shift],
            recv_sem=recv_sem.at[source],
            device_id=device(source),
            device_id_type=pl.DeviceIdType.MESH,
        )

    for shift in range(1, members):
        copy_to(shift).start()
    o_ref[me] = m_ref[pl.ds(pl.multiple_of(me * rows, rows), rows), :]
    for shift in range(1, members):
        source, landed = arrival(shift)
        landed.wait_recv()
        o_ref[source] = landing[source]
    for shift in range(1, members):
        copy_to(shift).wait_send()


def return_pieces(merged, members, collective_id=0):
    rows = merged.shape[0] // members
    piece = (members, rows, merged.shape[1])
    return pl.pallas_call(
        return_kernel,
        in_specs=[pl.BlockSpec(memory_space=pltpu.VMEM)],
        out_specs=pl.BlockSpec(memory_space=pltpu.VMEM),
        out_shape=jax.ShapeDtypeStruct(piece, merged.dtype),
        scratch_shapes=[
            pltpu.VMEM(piece, merged.dtype),
            pltpu.SemaphoreType.DMA((members,)),
            pltpu.SemaphoreType.DMA((members,)),
        ],
        compiler_params=pltpu.CompilerParams(collective_id=collective_id, has_side_effects=True),
    )(merged)


def shards(
    vertex_embeddings,
    adjacent_group_bank_ids,
    coupling_strength_panels,
    asking_projector,
    lookup_projector,
    content_projector,
    final_projector,
    passing_inner_coefficients,
    passing_outer_coefficients,
    softness_per_subspace,
    mixing_layer_gain,
):
    block_len = vertex_embeddings.shape[0]
    group_size = lax.axis_size("head")
    pair_size = lax.axis_size(PAIR)
    members = group_size * pair_size
    slot_ids = adjacent_group_bank_ids.reshape(-1)
    halo_rows = extended(vertex_embeddings, block_len)
    me = lax.axis_index("head")
    gathered = [halo_rows]
    for shift in range(1, group_size):
        pairs = [(i, (i + shift) % group_size) for i in range(group_size)]
        gathered.append(lax.ppermute(halo_rows, "head", pairs))
    stacked = jnp.stack(gathered)
    order = (me - jnp.arange(group_size)) % group_size
    nearby = jnp.zeros_like(stacked).at[order].set(stacked).reshape(-1, halo_rows.shape[1])
    slot_order = slot_ids.reshape(3, group_size).T.reshape(-1)
    asking_vector_multiplier = softness_per_subspace / math.sqrt(SUBSPACE_WIDTH)
    keys_all = head_norm(
        jnp.dot(vertex_embeddings, lookup_projector, preferred_element_type=jnp.float32), None
    )
    values_all = jnp.dot(
        vertex_embeddings, content_projector, preferred_element_type=jnp.float32
    ).astype(jnp.bfloat16)

    head_of = [(j % group_size) * pair_size + j // group_size for j in range(members)]
    member_of = [head_of.index(h) for h in range(NUM_SUBSPACES)]

    def to_members(parts):
        packed = jnp.stack(
            [t.reshape(block_len, NUM_SUBSPACES, SUBSPACE_WIDTH) for t in parts], axis=2
        )[:, jnp.array(head_of)]
        return lax.all_to_all(
            packed.reshape(block_len, -1), GROUP, split_axis=1, concat_axis=0, tiled=True
        )

    kv_packed = jnp.stack(
        [t.reshape(block_len, NUM_SUBSPACES, SUBSPACE_WIDTH) for t in (keys_all, values_all)],
        axis=2,
    )[:, jnp.array(head_of)]
    kv_pieces = jnp.transpose(kv_packed, (1, 0, 2, 3)).reshape(members * block_len, -1)
    key_values = return_pieces(kv_pieces, members, collective_id=1).reshape(members * block_len, -1)
    kv_in = lax.all_gather(key_values, (COLUMN, ROW), axis=0, tiled=True)
    queries = head_norm(
        jnp.dot(vertex_embeddings, asking_projector, preferred_element_type=jnp.float32),
        asking_vector_multiplier,
    )
    head_queries = to_members((queries,))
    query_rows = head_queries.shape[0]

    selected = jnp.take(coupling_strength_panels, jnp.maximum(slot_order, 0), axis=0)
    selected = jnp.where((slot_order >= 0)[:, None, None], selected, jnp.zeros_like(selected))
    wide_tiles = jnp.transpose(selected, (1, 0, 2)).reshape(block_len, -1)
    aggregate = jnp.dot(wide_tiles, nearby, preferred_element_type=jnp.float32).astype(jnp.bfloat16)
    hidden = jax.nn.gelu(
        jnp.dot(aggregate, passing_inner_coefficients, preferred_element_type=jnp.float32)
    ).astype(jnp.bfloat16)
    local_term = jnp.dot(hidden, passing_outer_coefficients, preferred_element_type=jnp.float32)

    local_term, head_queries = lax.optimization_barrier((local_term, head_queries))
    padded_queries = jnp.concatenate([head_queries, jnp.zeros_like(head_queries)], axis=1)
    merged = attend(padded_queries, kv_in)
    back = return_pieces(merged, members)
    node_heads = jnp.transpose(back, (1, 0, 2))[:, jnp.array(member_of)]
    node_heads = node_heads.reshape(block_len, -1)
    attended = jnp.dot(node_heads, final_projector, preferred_element_type=jnp.float32)
    normed = (
        attended
        * lax.rsqrt(jnp.mean(attended * attended, axis=-1, keepdims=True) + norm_eps)
        * mixing_layer_gain
    )
    return (vertex_embeddings.astype(jnp.float32) + local_term + normed).astype(jnp.bfloat16)


def solution(mesh):
    n_dom, n_head = mesh.shape["dom"], mesh.shape["head"]
    fine = Mesh(mesh.devices.reshape(n_dom // 16, 8, 2, n_head), (ROW, COLUMN, PAIR, "head"))
    in_specs = (
        P((ROW, COLUMN, PAIR, "head"), None),
        P(DOM, "head", None),
        P(),
        P(),
        P(),
        P(),
        P(),
        P(),
        P(),
        P(),
        P(),
    )
    out_specs = P((ROW, COLUMN, PAIR, "head"), None)
    return jax.shard_map(shards, mesh=fine, in_specs=in_specs, out_specs=out_specs, check_vma=False)
```

```python
import math

import jax
from jax.experimental import pallas as pl
from jax.experimental.pallas import tpu as pltpu
import jax.numpy as jnp
from jax import lax
from jax.sharding import Mesh
from jax.sharding import PartitionSpec as P

NUM_SUBSPACES = 8
SUBSPACE_WIDTH = 64
KEY_BLOCK = 8192
KEY_STEP = 4096
QUERY_STEP = 1024

norm_eps = 1e-06

ROW = "x"
COLUMN = "z"
PAIR = "yhi"
DOM = (ROW, COLUMN, PAIR)
GROUP = (PAIR, "head")


def extended(shard, width):
    devices = lax.axis_size(ROW) * lax.axis_size(COLUMN) * lax.axis_size(PAIR)
    length = shard.shape[0]
    up = [(i, (i + 1) % devices) for i in range(devices - 1)]
    down = [(j, i) for i, j in up]
    last = lax.slice_in_dim(shard, length - width, length, axis=0)
    first = lax.slice_in_dim(shard, 0, width, axis=0)
    before = lax.ppermute(last, DOM, up)
    after = lax.ppermute(first, DOM, down)
    return jnp.concatenate([before, shard, after], axis=0)


def head_norm(projected, scales):
    rows = projected.shape[0]
    grouped = projected.reshape(rows, -1, SUBSPACE_WIDTH)
    mean_square = jnp.mean(grouped * grouped, axis=-1, keepdims=True)
    scaled = grouped * lax.rsqrt(mean_square + norm_eps)
    if scales is not None:
        scaled = scaled * scales[None, :, None]
    return scaled.reshape(rows, -1).astype(jnp.bfloat16)


def attention_kernel(q_ref, kv_ref, o_ref, acc_ref):
    @pl.when(pl.program_id(0) == 0)
    def _():
        acc_ref[...] = jnp.zeros_like(acc_ref)

    q_step = min(QUERY_STEP, q_ref.shape[0])
    k_step = min(KEY_STEP, kv_ref.shape[0])
    q_count = q_ref.shape[0] // q_step
    k_count = kv_ref.shape[0] // k_step

    def body(turn, carry):
        rows = pl.ds(pl.multiple_of((turn // k_count) * q_step, q_step), q_step)
        keys = pl.ds(pl.multiple_of((turn % k_count) * k_step, k_step), k_step)
        block = kv_ref[keys, :]
        scores = lax.dot_general(
            q_ref[rows, :], block, (((1,), (1,)), ((), ())), preferred_element_type=jnp.float32
        )
        weights = jnp.exp(scores).astype(jnp.bfloat16)
        lane = lax.broadcasted_iota(jnp.int32, block.shape, 1)
        widened = jnp.where(lane < SUBSPACE_WIDTH, jnp.ones_like(block), block)
        acc_ref[rows, :] += jnp.dot(weights, widened, preferred_element_type=jnp.float32)
        return carry

    lax.fori_loop(0, q_count * k_count, body, 0)

    @pl.when(pl.program_id(0) == pl.num_programs(0) - 1)
    def _():
        totals = acc_ref[...]
        o_ref[...] = (totals[:, SUBSPACE_WIDTH:] / totals[:, :1]).astype(o_ref.dtype)


def attend(padded_queries, key_values):
    rows, width = padded_queries.shape
    keys = key_values.shape[0]
    block = min(KEY_BLOCK, keys)
    flops = 4 * rows * keys * width
    return pl.pallas_call(
        attention_kernel,
        grid=(keys // block,),
        in_specs=[
            pl.BlockSpec((rows, width), lambda j: (0, 0)),
            pl.BlockSpec((block, width), lambda j: (j, 0)),
        ],
        out_specs=pl.BlockSpec((rows, SUBSPACE_WIDTH), lambda j: (0, 0)),
        out_shape=jax.ShapeDtypeStruct((rows, SUBSPACE_WIDTH), jnp.bfloat16),
        scratch_shapes=[pltpu.VMEM((rows, width), jnp.float32)],
        compiler_params=pltpu.CompilerParams(dimension_semantics=("arbitrary",)),
        cost_estimate=pl.CostEstimate(
            flops=flops, transcendentals=rows * keys, bytes_accessed=2 * keys * width + 6 * rows * width
        ),
    )(padded_queries, key_values)


def return_kernel(m_ref, o_ref, landing, send_sem, recv_sem):
    group_size = lax.axis_size("head")
    members = lax.axis_size(PAIR) * group_size
    me = lax.axis_index(PAIR) * group_size + lax.axis_index("head")
    row = lax.axis_index(ROW)
    column = lax.axis_index(COLUMN)
    rows = o_ref.shape[0]

    def device(t):
        return (row, column, t // group_size, lax.rem(t, group_size))

    barrier = pltpu.get_barrier_semaphore()
    for shift in range(1, members):
        pl.semaphore_signal(
            barrier, inc=1, device_id=device(lax.rem(me + shift, members)),
            device_id_type=pl.DeviceIdType.MESH,
        )
    pl.semaphore_wait(barrier, members - 1)

    def copy_to(shift):
        target = lax.rem(me + shift, members)
        return pltpu.make_async_remote_copy(
            src_ref=m_ref.at[pl.ds(pl.multiple_of(target * rows, rows), rows)],
            dst_ref=landing.at[me],
            send_sem=send_sem.at[shift],
            recv_sem=recv_sem.at[me],
            device_id=device(target),
            device_id_type=pl.DeviceIdType.MESH,
        )

    def arrival(shift):
        source = lax.rem(me - shift + members, members)
        return source, pltpu.make_async_remote_copy(
            src_ref=m_ref.at[pl.ds(0, rows)],
            dst_ref=landing.at[source],
            send_sem=send_sem.at[shift],
            recv_sem=recv_sem.at[source],
            device_id=device(source),
            device_id_type=pl.DeviceIdType.MESH,
        )

    for shift in range(1, members):
        copy_to(shift).start()
    landing[me] = m_ref[pl.ds(pl.multiple_of(me * rows, rows), rows), :]
    for shift in range(1, members):
        landed = arrival(shift)[1]
        landed.wait_recv()
    width = m_ref.shape[1]
    for j in range(members):
        head = (j % group_size) * (members // group_size) + j // group_size
        o_ref[:, head * width : (head + 1) * width] = landing[j]
    for shift in range(1, members):
        copy_to(shift).wait_send()


def return_pieces(merged, members):
    rows = merged.shape[0] // members
    piece = (members, rows, merged.shape[1])
    return pl.pallas_call(
        return_kernel,
        in_specs=[pl.BlockSpec(memory_space=pltpu.VMEM)],
        out_specs=pl.BlockSpec(memory_space=pltpu.VMEM),
        out_shape=jax.ShapeDtypeStruct((rows, members * merged.shape[1]), merged.dtype),
        scratch_shapes=[
            pltpu.VMEM(piece, merged.dtype),
            pltpu.SemaphoreType.DMA((members,)),
            pltpu.SemaphoreType.DMA((members,)),
        ],
        compiler_params=pltpu.CompilerParams(collective_id=0, has_side_effects=True),
    )(merged)


def shards(
    vertex_embeddings,
    adjacent_group_bank_ids,
    coupling_strength_panels,
    asking_projector,
    lookup_projector,
    content_projector,
    final_projector,
    passing_inner_coefficients,
    passing_outer_coefficients,
    softness_per_subspace,
    mixing_layer_gain,
):
    block_len = vertex_embeddings.shape[0]
    group_size = lax.axis_size("head")
    pair_size = lax.axis_size(PAIR)
    members = group_size * pair_size
    slot_ids = adjacent_group_bank_ids.reshape(-1)
    halo_rows = extended(vertex_embeddings, block_len)
    me = lax.axis_index("head")
    gathered = [halo_rows]
    for shift in range(1, group_size):
        pairs = [(i, (i + shift) % group_size) for i in range(group_size)]
        gathered.append(lax.ppermute(halo_rows, "head", pairs))
    stacked = jnp.stack(gathered)
    order = (me - jnp.arange(group_size)) % group_size
    nearby = jnp.zeros_like(stacked).at[order].set(stacked).reshape(-1, halo_rows.shape[1])
    slot_order = slot_ids.reshape(3, group_size).T.reshape(-1)
    asking_vector_multiplier = softness_per_subspace / math.sqrt(SUBSPACE_WIDTH)
    keys_all = head_norm(
        jnp.dot(vertex_embeddings, lookup_projector, preferred_element_type=jnp.float32), None
    )
    values_all = jnp.dot(
        vertex_embeddings, content_projector, preferred_element_type=jnp.float32
    ).astype(jnp.bfloat16)

    head_of = [(j % group_size) * pair_size + j // group_size for j in range(members)]
    member_of = [head_of.index(h) for h in range(NUM_SUBSPACES)]

    def to_members(parts):
        packed = jnp.stack(
            [t.reshape(block_len, NUM_SUBSPACES, SUBSPACE_WIDTH) for t in parts], axis=2
        )[:, jnp.array(head_of)]
        return lax.all_to_all(
            packed.reshape(block_len, -1), GROUP, split_axis=1, concat_axis=0, tiled=True
        )

    key_values = to_members((keys_all, values_all))
    kv_in = lax.all_gather(key_values, (COLUMN, ROW), axis=0, tiled=True)
    queries = head_norm(
        jnp.dot(vertex_embeddings, asking_projector, preferred_element_type=jnp.float32),
        asking_vector_multiplier,
    )
    head_queries = to_members((queries,))
    query_rows = head_queries.shape[0]

    selected = jnp.take(coupling_strength_panels, jnp.maximum(slot_order, 0), axis=0)
    selected = jnp.where((slot_order >= 0)[:, None, None], selected, jnp.zeros_like(selected))
    wide_tiles = jnp.transpose(selected, (1, 0, 2)).reshape(block_len, -1)
    aggregate = jnp.dot(wide_tiles, nearby, preferred_element_type=jnp.float32).astype(jnp.bfloat16)
    hidden = jax.nn.gelu(
        jnp.dot(aggregate, passing_inner_coefficients, preferred_element_type=jnp.float32)
    ).astype(jnp.bfloat16)
    local_term = jnp.dot(hidden, passing_outer_coefficients, preferred_element_type=jnp.float32)

    local_term, head_queries = lax.optimization_barrier((local_term, head_queries))
    padded_queries = jnp.concatenate([head_queries, jnp.zeros_like(head_queries)], axis=1)
    merged = attend(padded_queries, kv_in)
    node_heads = return_pieces(merged, members)
    node_heads = node_heads.reshape(block_len, -1)
    attended = jnp.dot(node_heads, final_projector, preferred_element_type=jnp.float32)
    normed = (
        attended
        * lax.rsqrt(jnp.mean(attended * attended, axis=-1, keepdims=True) + norm_eps)
        * mixing_layer_gain
    )
    return (vertex_embeddings.astype(jnp.float32) + local_term + normed).astype(jnp.bfloat16)


def solution(mesh):
    n_dom, n_head = mesh.shape["dom"], mesh.shape["head"]
    fine = Mesh(mesh.devices.reshape(n_dom // 16, 8, 2, n_head), (ROW, COLUMN, PAIR, "head"))
    in_specs = (
        P((ROW, COLUMN, PAIR, "head"), None),
        P(DOM, "head", None),
        P(),
        P(),
        P(),
        P(),
        P(),
        P(),
        P(),
        P(),
        P(),
    )
    out_specs = P((ROW, COLUMN, PAIR, "head"), None)
    return jax.shard_map(shards, mesh=fine, in_specs=in_specs, out_specs=out_specs, check_vma=False)
```

```python
import math

import jax
from jax.experimental import pallas as pl
from jax.experimental.pallas import tpu as pltpu
import jax.numpy as jnp
from jax import lax
from jax.sharding import Mesh
from jax.sharding import PartitionSpec as P

NUM_SUBSPACES = 8
SUBSPACE_WIDTH = 64
KEY_BLOCK = 8192
KEY_STEP = 4096
QUERY_STEP = 1024

norm_eps = 1e-06

ROW = "x"
COLUMN = "z"
PAIR = "yhi"
DOM = (ROW, COLUMN, PAIR)
GROUP = (PAIR, "head")


def extended(shard, width):
    devices = lax.axis_size(ROW) * lax.axis_size(COLUMN) * lax.axis_size(PAIR)
    length = shard.shape[0]
    up = [(i, (i + 1) % devices) for i in range(devices - 1)]
    down = [(j, i) for i, j in up]
    last = lax.slice_in_dim(shard, length - width, length, axis=0)
    first = lax.slice_in_dim(shard, 0, width, axis=0)
    before = lax.ppermute(last, DOM, up)
    after = lax.ppermute(first, DOM, down)
    return jnp.concatenate([before, shard, after], axis=0)


def head_norm(projected, scales):
    rows = projected.shape[0]
    grouped = projected.reshape(rows, -1, SUBSPACE_WIDTH)
    mean_square = jnp.mean(grouped * grouped, axis=-1, keepdims=True)
    scaled = grouped * lax.rsqrt(mean_square + norm_eps)
    if scales is not None:
        scaled = scaled * scales[None, :, None]
    return scaled.reshape(rows, -1).astype(jnp.bfloat16)


def attention_kernel(q_ref, kv_ref, o_ref, acc_ref):
    @pl.when(pl.program_id(0) == 0)
    def _():
        acc_ref[...] = jnp.zeros_like(acc_ref)

    q_step = min(QUERY_STEP, q_ref.shape[0])
    k_step = min(KEY_STEP, kv_ref.shape[0])
    q_count = q_ref.shape[0] // q_step
    k_count = kv_ref.shape[0] // k_step

    def body(turn, carry):
        rows = pl.ds(pl.multiple_of((turn // k_count) * q_step, q_step), q_step)
        keys = pl.ds(pl.multiple_of((turn % k_count) * k_step, k_step), k_step)
        block = kv_ref[keys, :]
        scores = lax.dot_general(
            q_ref[rows, :], block, (((1,), (1,)), ((), ())), preferred_element_type=jnp.float32
        )
        weights = jnp.exp(scores).astype(jnp.bfloat16)
        lane = lax.broadcasted_iota(jnp.int32, block.shape, 1)
        widened = jnp.where(lane < SUBSPACE_WIDTH, jnp.ones_like(block), block)
        acc_ref[rows, :] += jnp.dot(weights, widened, preferred_element_type=jnp.float32)
        return carry

    lax.fori_loop(0, q_count * k_count, body, 0)

    @pl.when(pl.program_id(0) == pl.num_programs(0) - 1)
    def _():
        totals = acc_ref[...]
        o_ref[...] = (totals[:, SUBSPACE_WIDTH:] / totals[:, :1]).astype(o_ref.dtype)


def attend(padded_queries, key_values):
    rows, width = padded_queries.shape
    keys = key_values.shape[0]
    block = min(KEY_BLOCK, keys)
    flops = 4 * rows * keys * width
    return pl.pallas_call(
        attention_kernel,
        grid=(keys // block,),
        in_specs=[
            pl.BlockSpec((rows, width), lambda j: (0, 0)),
            pl.BlockSpec((block, width), lambda j: (j, 0)),
        ],
        out_specs=pl.BlockSpec((rows, SUBSPACE_WIDTH), lambda j: (0, 0)),
        out_shape=jax.ShapeDtypeStruct((rows, SUBSPACE_WIDTH), jnp.bfloat16),
        scratch_shapes=[pltpu.VMEM((rows, width), jnp.float32)],
        compiler_params=pltpu.CompilerParams(dimension_semantics=("arbitrary",)),
        cost_estimate=pl.CostEstimate(
            flops=flops, transcendentals=rows * keys, bytes_accessed=2 * keys * width + 6 * rows * width
        ),
    )(padded_queries, key_values)


def return_kernel(m_ref, o_ref, landing, send_sem, recv_sem):
    group_size = lax.axis_size("head")
    members = lax.axis_size(PAIR) * group_size
    me = lax.axis_index(PAIR) * group_size + lax.axis_index("head")
    row = lax.axis_index(ROW)
    column = lax.axis_index(COLUMN)
    rows = o_ref.shape[0]

    def device(t):
        return (row, column, t // group_size, lax.rem(t, group_size))

    barrier = pltpu.get_barrier_semaphore()
    for shift in range(1, members):
        pl.semaphore_signal(
            barrier, inc=1, device_id=device(lax.rem(me + shift, members)),
            device_id_type=pl.DeviceIdType.MESH,
        )
    pl.semaphore_wait(barrier, members - 1)

    def copy_to(shift):
        target = lax.rem(me + shift, members)
        return pltpu.make_async_remote_copy(
            src_ref=m_ref.at[pl.ds(pl.multiple_of(target * rows, rows), rows)],
            dst_ref=landing.at[me],
            send_sem=send_sem.at[shift],
            recv_sem=recv_sem.at[me],
            device_id=device(target),
            device_id_type=pl.DeviceIdType.MESH,
        )

    def arrival(shift):
        source = lax.rem(me - shift + members, members)
        return source, pltpu.make_async_remote_copy(
            src_ref=m_ref.at[pl.ds(0, rows)],
            dst_ref=landing.at[source],
            send_sem=send_sem.at[shift],
            recv_sem=recv_sem.at[source],
            device_id=device(source),
            device_id_type=pl.DeviceIdType.MESH,
        )

    for shift in range(1, members):
        copy_to(shift).start()
    landing[me] = m_ref[pl.ds(pl.multiple_of(me * rows, rows), rows), :]
    for shift in range(1, members):
        landed = arrival(shift)[1]
        landed.wait_recv()
    width = m_ref.shape[1]
    for j in range(members):
        head = (j % group_size) * (members // group_size) + j // group_size
        o_ref[:, head * width : (head + 1) * width] = landing[j]
    for shift in range(1, members):
        copy_to(shift).wait_send()


def return_pieces(merged, members, collective_id=0):
    rows = merged.shape[0] // members
    piece = (members, rows, merged.shape[1])
    return pl.pallas_call(
        return_kernel,
        in_specs=[pl.BlockSpec(memory_space=pltpu.VMEM)],
        out_specs=pl.BlockSpec(memory_space=pltpu.VMEM),
        out_shape=jax.ShapeDtypeStruct((rows, members * merged.shape[1]), merged.dtype),
        scratch_shapes=[
            pltpu.VMEM(piece, merged.dtype),
            pltpu.SemaphoreType.DMA((members,)),
            pltpu.SemaphoreType.DMA((members,)),
        ],
        compiler_params=pltpu.CompilerParams(collective_id=collective_id, has_side_effects=True),
    )(merged)


def shards(
    vertex_embeddings,
    adjacent_group_bank_ids,
    coupling_strength_panels,
    asking_projector,
    lookup_projector,
    content_projector,
    final_projector,
    passing_inner_coefficients,
    passing_outer_coefficients,
    softness_per_subspace,
    mixing_layer_gain,
):
    block_len = vertex_embeddings.shape[0]
    group_size = lax.axis_size("head")
    pair_size = lax.axis_size(PAIR)
    members = group_size * pair_size
    slot_ids = adjacent_group_bank_ids.reshape(-1)
    halo_rows = extended(vertex_embeddings, block_len)
    me = lax.axis_index("head")
    gathered = [halo_rows]
    for shift in range(1, group_size):
        pairs = [(i, (i + shift) % group_size) for i in range(group_size)]
        gathered.append(lax.ppermute(halo_rows, "head", pairs))
    stacked = jnp.stack(gathered)
    order = (me - jnp.arange(group_size)) % group_size
    nearby = jnp.zeros_like(stacked).at[order].set(stacked).reshape(-1, halo_rows.shape[1])
    slot_order = slot_ids.reshape(3, group_size).T.reshape(-1)
    asking_vector_multiplier = softness_per_subspace / math.sqrt(SUBSPACE_WIDTH)
    keys_all = head_norm(
        jnp.dot(vertex_embeddings, lookup_projector, preferred_element_type=jnp.float32), None
    )
    values_all = jnp.dot(
        vertex_embeddings, content_projector, preferred_element_type=jnp.float32
    ).astype(jnp.bfloat16)

    head_of = [(j % group_size) * pair_size + j // group_size for j in range(members)]
    member_of = [head_of.index(h) for h in range(NUM_SUBSPACES)]

    def to_members(parts):
        packed = jnp.stack(
            [t.reshape(block_len, NUM_SUBSPACES, SUBSPACE_WIDTH) for t in parts], axis=2
        )[:, jnp.array(head_of)]
        return lax.all_to_all(
            packed.reshape(block_len, -1), GROUP, split_axis=1, concat_axis=0, tiled=True
        )

    kv_packed = jnp.stack(
        [t.reshape(block_len, NUM_SUBSPACES, SUBSPACE_WIDTH) for t in (keys_all, values_all)],
        axis=2,
    )[:, jnp.array(head_of)]
    kv_pieces = jnp.transpose(kv_packed, (1, 0, 2, 3)).reshape(members * block_len, -1)
    key_values = return_pieces(kv_pieces, members, collective_id=1).reshape(members * block_len, -1)
    kv_in = lax.all_gather(key_values, (COLUMN, ROW), axis=0, tiled=True)
    queries = head_norm(
        jnp.dot(vertex_embeddings, asking_projector, preferred_element_type=jnp.float32),
        asking_vector_multiplier,
    )
    head_queries = to_members((queries,))
    query_rows = head_queries.shape[0]

    selected = jnp.take(coupling_strength_panels, jnp.maximum(slot_order, 0), axis=0)
    selected = jnp.where((slot_order >= 0)[:, None, None], selected, jnp.zeros_like(selected))
    wide_tiles = jnp.transpose(selected, (1, 0, 2)).reshape(block_len, -1)
    aggregate = jnp.dot(wide_tiles, nearby, preferred_element_type=jnp.float32).astype(jnp.bfloat16)
    hidden = jax.nn.gelu(
        jnp.dot(aggregate, passing_inner_coefficients, preferred_element_type=jnp.float32)
    ).astype(jnp.bfloat16)
    local_term = jnp.dot(hidden, passing_outer_coefficients, preferred_element_type=jnp.float32)

    local_term, head_queries = lax.optimization_barrier((local_term, head_queries))
    padded_queries = jnp.concatenate([head_queries, jnp.zeros_like(head_queries)], axis=1)
    merged = attend(padded_queries, kv_in)
    node_heads = return_pieces(merged, members)
    node_heads = node_heads.reshape(block_len, -1)
    attended = jnp.dot(node_heads, final_projector, preferred_element_type=jnp.float32)
    normed = (
        attended
        * lax.rsqrt(jnp.mean(attended * attended, axis=-1, keepdims=True) + norm_eps)
        * mixing_layer_gain
    )
    return (vertex_embeddings.astype(jnp.float32) + local_term + normed).astype(jnp.bfloat16)


def solution(mesh):
    n_dom, n_head = mesh.shape["dom"], mesh.shape["head"]
    fine = Mesh(mesh.devices.reshape(n_dom // 16, 8, 2, n_head), (ROW, COLUMN, PAIR, "head"))
    in_specs = (
        P((ROW, COLUMN, PAIR, "head"), None),
        P(DOM, "head", None),
        P(),
        P(),
        P(),
        P(),
        P(),
        P(),
        P(),
        P(),
        P(),
    )
    out_specs = P((ROW, COLUMN, PAIR, "head"), None)
    return jax.shard_map(shards, mesh=fine, in_specs=in_specs, out_specs=out_specs, check_vma=False)
```
